512 devices in a mesh: chan: 16 (over y_hi, x, core), tm: 32 (over z, y_lo).
Axes of the slice: x: 4, y: 4 (y_hi: 2, y_lo: 2; y = y_hi * 2 + y_lo), z: 16, core: 2. Of those that a mesh axis runs over, the one named last changes fastest.
Arguments:
- ref_signal: float32 [2, 65536], P(None, 'tm'), may hold values from -40 to 40
- surveillance: float32 [2, 256, 65536], P(None, 'chan', 'tm'), may hold values from -2000 to 2000
- steering: float32 [2, 64, 256], P(None, None, 'chan'), may hold values from -0.5 to 0.5
Outputs:
- range_doppler: float32 [64, 2, 256, 256], P('chan', None, 'tm')
The draws below stay inside these ranges and needn't reach their ends.
All inputs are finite; a program needn't handle non-finite values.
Results may differ from the reference program's by a relative error of at most 0.0003.
Values sent between devices are 32-bit elements; how exact they have to be, the bound alone decides.
A program may use at most 64 MiB of HBM per device.

```python
import math
import jax
import jax.numpy as jnp
from jax import lax

CHANNELS = 256
BEAMS = 64
LAGS = 256
DOPPLER = 256
TAPS = 64
BLOCK_LEN = 256
SAMPLES = 65536


def make_signals(key):
    base_key = jax.random.fold_in(key, 4242)
    keys = jax.random.split(base_key, 5)
    base = jnp.clip(jax.random.normal(keys[0], (2, SAMPLES), jnp.float32), -5.0, 5.0) * math.sqrt(0.5)
    fades = jnp.exp(jax.random.uniform(keys[1], (SAMPLES // 32,), jnp.float32, 0.0, math.log(3.2)))
    fading = jnp.repeat(fades, 32)
    ramp = jnp.arange(SAMPLES, dtype=jnp.float32) / SAMPLES
    trend = 1.0 + 0.75 * ramp
    ref_signal = base * fading * trend
    reach = max(TAPS // 4, 1)
    clutter_taps = jnp.clip(jax.random.normal(keys[2], (2, CHANNELS, reach), jnp.float32), -4.0, 4.0) * (1.5 / math.sqrt(reach))
    clutter_real = jnp.zeros((CHANNELS, SAMPLES), jnp.float32)
    clutter_imag = jnp.zeros((CHANNELS, SAMPLES), jnp.float32)
    for delay in range(reach):
        shifted = jnp.pad(ref_signal, ((0, 0), (delay, 0)))[:, :SAMPLES]
        tap_real = clutter_taps[0, :, delay:delay + 1]
        tap_imag = clutter_taps[1, :, delay:delay + 1]
        clutter_real = clutter_real + tap_real * shifted[0][None, :] - tap_imag * shifted[1][None, :]
        clutter_imag = clutter_imag + tap_real * shifted[1][None, :] + tap_imag * shifted[0][None, :]
    levels = jnp.exp(jax.random.uniform(keys[3], (CHANNELS, 1), jnp.float32, 0.0, math.log(3.2)))
    noise = jnp.clip(jax.random.normal(keys[4], (2, CHANNELS, SAMPLES), jnp.float32), -5.0, 5.0) * math.sqrt(0.5)
    surveillance = jnp.stack([clutter_real, clutter_imag], 0) + noise * levels[None, :, :]
    return (ref_signal, surveillance)


def draw_ref_signal(key, part):
    return make_signals(key)[0]


def draw_surveillance(key, part):
    return make_signals(key)[1]


def spiked(result, stream_key, source, target, blocks, factor):
    def block_of(dim):
        return (jnp.arange(result.shape[dim]) // (result.shape[dim] // blocks)).reshape((-1,) + (1,) * (result.ndim - 1 - dim))

    near = jax.random.permutation(stream_key, blocks)[block_of(target)]
    other_side = (block_of(target) + blocks // 2) % blocks
    return jnp.where((block_of(source) == near) | (block_of(source) == other_side), factor * result, result)


def block_levels(rng, dims, shards, smallest, high):
    def one(position, blocks):
        steps = jax.random.uniform(jax.random.fold_in(jax.random.fold_in(rng, 6), position), (blocks,), jnp.float32, smallest / len(shards), high / len(shards))
        return jnp.repeat(jnp.exp(steps), dims[position] // blocks).reshape((-1,) + (1,) * (len(dims) - position - 1))

    level = one(*shards[0])
    for cut in shards[1:]:
        level = level * one(*cut)
    return level


def noise_with(rng, extent, spread, bound, cuts, heavy, kind=jnp.bfloat16):
    array = spread * jax.random.normal(rng, extent, jnp.float32)
    if cuts:
        array = array * block_levels(rng, extent, cuts, -0.22, 0.18)
    return jnp.clip(spiked(array, jax.random.fold_in(rng, 3), *heavy), -bound, bound).astype(kind)


def setup_inputs(seed: int = 0) -> dict:
    streams_of = jax.random.split(jax.random.key(seed), 4)
    return {
        "ref_signal": draw_ref_signal(jax.random.fold_in(streams_of[3], 71), 0),
        "surveillance": draw_surveillance(jax.random.fold_in(streams_of[3], 71), 0),
        "steering": noise_with(streams_of[2], (2, BEAMS, CHANNELS), CHANNELS ** -0.5, 0.5, ((2, 16),), (2, 1, 16, 2.0), jnp.float32),
    }


def lag_window(ref_ext, offset):
    window = lax.dynamic_slice_in_dim(ref_ext, offset, BLOCK_LEN + LAGS, 1)
    positions = (jnp.arange(BLOCK_LEN)[None, :] - jnp.arange(LAGS)[:, None] + LAGS).astype(jnp.int32)
    return window[:, positions]

def reference(ref_signal, surveillance, steering):
    highest = lax.Precision.HIGHEST
    blocks_all = SAMPLES // BLOCK_LEN
    ref_ext = jnp.concatenate([jnp.zeros((2, LAGS), jnp.float32), ref_signal], axis=1)
    survey = surveillance.reshape(2 * CHANNELS, SAMPLES)
    block_ids = jnp.arange(blocks_all, dtype=jnp.int32)

    def statistics(carry, block_idx):
        offset = (block_idx * BLOCK_LEN).astype(jnp.int32)
        basis = lag_window(ref_ext, offset)[:, :TAPS, :].reshape(2 * TAPS, BLOCK_LEN)
        portion = lax.dynamic_slice_in_dim(survey, offset, BLOCK_LEN, 1)
        gram_sum = carry[0] + jnp.dot(basis, basis.T, precision=highest)
        cross_sum = carry[1] + jnp.dot(basis, portion.T, precision=highest)
        return ((gram_sum, cross_sum), None)
    start_carry = (jnp.zeros((2 * TAPS, 2 * TAPS), jnp.float32), jnp.zeros((2 * TAPS, 2 * CHANNELS), jnp.float32))
    (gram_sum, cross_sum), _ = lax.scan(statistics, start_carry, block_ids)
    g_real = gram_sum[:TAPS, :TAPS] + gram_sum[TAPS:, TAPS:]
    g_imag = gram_sum[:TAPS, TAPS:] - gram_sum[TAPS:, :TAPS]
    system = jnp.concatenate([jnp.concatenate([g_real, -g_imag], 1), jnp.concatenate([g_imag, g_real], 1)], 0)
    b_real = cross_sum[:TAPS, :CHANNELS] + cross_sum[TAPS:, CHANNELS:]
    b_imag = cross_sum[:TAPS, CHANNELS:] - cross_sum[TAPS:, :CHANNELS]
    solved = jnp.linalg.solve(system, jnp.concatenate([b_real, b_imag], 0))
    a_real = solved[:TAPS].T
    a_imag = solved[TAPS:].T
    mixing = jnp.concatenate([jnp.concatenate([a_real, -a_imag], 1), jnp.concatenate([a_imag, a_real], 1)], 0)

    def cleanse(carry, block_idx):
        offset = (block_idx * BLOCK_LEN).astype(jnp.int32)
        basis = lag_window(ref_ext, offset)[:, :TAPS, :].reshape(2 * TAPS, BLOCK_LEN)
        portion = lax.dynamic_slice_in_dim(survey, offset, BLOCK_LEN, 1)
        return (carry, portion - jnp.dot(mixing, basis, precision=highest))
    _, cleaned_blocks = lax.scan(cleanse, None, block_ids)
    cleaned = cleaned_blocks.transpose(1, 0, 2).reshape(2 * CHANNELS, SAMPLES)
    w_real = steering[0]
    w_imag = steering[1]
    w_big = jnp.concatenate([jnp.concatenate([w_real, -w_imag], 1), jnp.concatenate([w_imag, w_real], 1)], 0)
    beams = jnp.dot(w_big, cleaned, precision=highest)

    def correlate(carry, block_idx):
        offset = (block_idx * BLOCK_LEN).astype(jnp.int32)
        lag_rows = lag_window(ref_ext, offset).reshape(2 * LAGS, BLOCK_LEN)
        segment = lax.dynamic_slice_in_dim(beams, offset, BLOCK_LEN, 1)
        product = jnp.dot(segment, lag_rows.T, precision=highest).reshape(2, BEAMS, 2, LAGS)
        real_part = product[0, :, 0] + product[1, :, 1]
        imag_part = product[1, :, 0] - product[0, :, 1]
        return (carry, jnp.stack([real_part, imag_part], 0))
    _, lagged = lax.scan(correlate, None, block_ids)
    spectrum = jnp.fft.fft(lax.complex(lagged[:, 0], lagged[:, 1]), n=DOPPLER, axis=0)
    stacked = jnp.stack([jnp.real(spectrum), jnp.imag(spectrum)], 0)
    scale = 0.125 / math.sqrt(SAMPLES)
    return stacked.transpose(2, 0, 3, 1) * scale
```

```python
import functools
import math

import jax
import jax.numpy as jnp
import numpy as np
from jax import lax
from jax.experimental import pallas as pl
from jax.experimental.pallas import tpu as pltpu
from jax.sharding import PartitionSpec as P

LAGS = 256
DOPPLER = 256
TAPS = 64
BLOCK = 256
HALO = 256
MESH = pl.DeviceIdType.MESH
HIGHEST = lax.Precision.HIGHEST


def dot(a, b):
    return lax.dot_general(a, b, (((1,), (0,)), ((), ())), precision=HIGHEST, preferred_element_type=jnp.float32)


def dot_nt(a, b):
    return lax.dot_general(a, b, (((1,), (1,)), ((), ())), precision=HIGHEST, preferred_element_type=jnp.float32)


def iota(shape, dim):
    return lax.broadcasted_iota(jnp.int32, shape, dim)


def conj_pack(a, b):
    half = a.shape[1] // 2
    sign = jnp.where(iota(a.shape, 1) < half, 1.0, -1.0)
    return sign * a + pltpu.roll(b, half, 1)


def widen(packed):
    half = packed.shape[1] // 2
    sign = jnp.where(iota(packed.shape, 1) < half, 1.0, -1.0)
    return jnp.concatenate([packed * sign, pltpu.roll(packed, half, 1)], 0)


def hermitian_inverse(m):
    n = m.shape[0]
    lane = iota((1, 2 * n), 1)
    row_id = iota((n, 1), 0)
    for k in range(n):
        col_re = m[:, k : k + 1]
        col_im = m[:, n + k : n + k + 1]
        row = m[k : k + 1, :]
        inv = 1.0 / m[k : k + 1, k : k + 1]
        here = (lane == k) | (lane == n + k)
        row = jnp.where(here, jnp.where(lane == k, 1.0, 0.0), row) * inv
        turned = pltpu.roll(row, n, 1) * jnp.where(lane < n, -1.0, 1.0)
        rest = jnp.where(here, 0.0, m) - col_re * row - col_im * turned
        m = jnp.where(row_id == k, row, rest)
    return m


def gram_matrix(g_row, e_row):
    n = TAPS
    row = iota((n, 2 * n), 0)
    lane = iota((n, 2 * n), 1)
    col = lane % n
    sign = jnp.where(lane < n, 1.0, -1.0)

    def shifted(v):
        return pltpu.roll(jnp.broadcast_to(v, (n, 2 * n)), 0, 1, stride=1, stride_axis=0)

    upper = jnp.where(col >= row, shifted(g_row), 0.0)
    flipped = jnp.concatenate([upper, jnp.zeros_like(upper)], 0).T
    lower = flipped[:n] - pltpu.roll(flipped[n:], n, 1)
    toeplitz = jnp.where(col >= row, upper, lower)
    tail = jnp.where((col >= row) & (row >= 1), shifted(e_row), 0.0)
    tail = jnp.concatenate([tail, jnp.zeros_like(tail)], 0)
    square = dot(tail.T, tail)
    return toeplitz - (square[:n] + sign * pltpu.roll(square[n:], n, 1))


def kernel(nc, nt, ref_ref, surv_ref, w_ref, table_ref, out_ref,
           part, rs_buf, halo, lagt, gm, gm_buf, xm, xm_buf, emb, lg, lg_buf,
           halo_ss, halo_rs, rs_ss, rs_rs, gm_ss, gm_rs, xm_ss, xm_rs, lg_ss, lg_rs):
    c = lax.axis_index("chan")
    d = lax.axis_index("tm")
    length = ref_ref.shape[1]
    beams = part.shape[1] // 2
    blocks = length // BLOCK

    def tm_peer(j):
        return lax.rem(d + nt // 2 + (1 - 2 * (j % 2)) * ((j + 1) // 2) + nt, nt)

    def chan_peer(j):
        return lax.rem(c + 1 + j, nc)

    barrier = pltpu.get_barrier_semaphore()

    def greet_chan(j, _):
        pl.semaphore_signal(barrier, inc=1, device_id={"chan": chan_peer(j)}, device_id_type=MESH)
        return 0

    def greet_tm(j, _):
        pl.semaphore_signal(barrier, inc=1, device_id={"tm": tm_peer(j)}, device_id_type=MESH)
        return 0

    lax.fori_loop(0, nt - 1, greet_tm, 0)
    lax.fori_loop(0, nc - 1, greet_chan, 0)

    partial = dot(w_ref[...], surv_ref[...])
    for dest in range(nc):
        part[dest] = partial[2 * beams * dest : 2 * beams * (dest + 1), :]

    pl.semaphore_wait(barrier, nt - 1 + nc - 1)

    right = lax.rem(d + 1, nt)
    halo_copy = pltpu.make_async_remote_copy(
        src_ref=ref_ref.at[:, pl.ds(length - HALO, HALO)], dst_ref=halo, send_sem=halo_ss, recv_sem=halo_rs,
        device_id={"tm": right}, device_id_type=MESH)
    halo_copy.start()

    def rs_copy(peer, slot):
        return pltpu.make_async_remote_copy(
            src_ref=part.at[peer], dst_ref=rs_buf.at[slot], send_sem=rs_ss.at[peer], recv_sem=rs_rs.at[slot],
            device_id={"chan": peer}, device_id_type=MESH)

    def rs_start(j, _):
        rs_copy(chan_peer(j), c).start()
        return 0

    lax.fori_loop(0, nc - 1, rs_start, 0)

    halo_copy.wait()
    ref = ref_ref[...]
    before = jnp.where(d == 0, 0.0, halo[...])
    extended = jnp.concatenate([before, ref], 1)
    for p in range(2):
        shifted = pltpu.roll(
            jnp.broadcast_to(extended[p : p + 1, :], (LAGS, HALO + length)), 0, 1, stride=1, stride_axis=0)
        lagt[p] = shifted[:, HALO:]
    taps = jnp.concatenate([lagt[0, :TAPS, :], lagt[1, :TAPS, :]], 0)

    row8 = iota((8, length), 0)
    mark = jnp.where((iota((8, length), 1) == length - 1) & (d == nt - 1), 1.0, 0.0)
    probe = jnp.where(row8 == 0, ref[0:1], jnp.where(row8 == 1, ref[1:2], jnp.where(row8 == 2, mark, 0.0)))
    g_raw = dot_nt(probe, taps)
    g_conj = conj_pack(g_raw[0:1], g_raw[1:2])
    gm[0:1, :] = jnp.where(iota(g_conj.shape, 1) < TAPS, g_conj, -g_conj)
    gm[1:2, :] = g_raw[2:3]

    def gm_copy(peer, slot):
        return pltpu.make_async_remote_copy(
            src_ref=gm, dst_ref=gm_buf.at[slot], send_sem=gm_ss.at[peer], recv_sem=gm_rs.at[slot],
            device_id={"tm": peer}, device_id_type=MESH)

    def xm_copy(peer, slot):
        return pltpu.make_async_remote_copy(
            src_ref=xm, dst_ref=xm_buf.at[slot], send_sem=xm_ss.at[peer], recv_sem=xm_rs.at[slot],
            device_id={"tm": peer}, device_id_type=MESH)

    def lg_copy(peer, slot):
        return pltpu.make_async_remote_copy(
            src_ref=lg.at[peer], dst_ref=lg_buf.at[slot], send_sem=lg_ss.at[peer], recv_sem=lg_rs.at[slot],
            device_id={"tm": peer}, device_id_type=MESH)

    def tm_start(copy):
        def body(j, _):
            copy(tm_peer(j), d).start()
            return 0

        lax.fori_loop(0, nt - 1, body, 0)

    def tm_wait_recv(copy):
        def body(j, _):
            peer = tm_peer(j)
            copy(peer, peer).wait_recv()
            return 0

        lax.fori_loop(0, nt - 1, body, 0)

    def tm_wait_send(copy):
        def body(j, _):
            peer = tm_peer(j)
            copy(peer, peer).wait_send()
            return 0

        lax.fori_loop(0, nt - 1, body, 0)

    tm_start(gm_copy)
    gm_buf[d] = gm[...]

    def rs_wait(j, _):
        peer = chan_peer(j)
        rs_copy(peer, peer).wait_recv()
        return 0

    lax.fori_loop(0, nc - 1, rs_wait, 0)
    rs_buf[c] = part[c]
    total = rs_buf[0]
    for source in range(1, nc):
        total = total + rs_buf[source]

    x_raw = dot_nt(total, taps)
    xm[...] = conj_pack(x_raw[:beams], x_raw[beams:])
    tm_start(xm_copy)
    xm_buf[d] = xm[...]

    tm_wait_recv(gm_copy)
    g_sum = jnp.sum(gm_buf[...], axis=0)
    gram = gram_matrix(g_sum[0:1], g_sum[1:2])
    inverse = widen(hermitian_inverse(gram))
    gram_wide = widen(gram)

    tm_wait_recv(xm_copy)
    x = jnp.sum(xm_buf[...], axis=0)
    weights = dot(x, inverse)
    weights = weights + dot(x - dot(weights, gram_wide), inverse)

    sign = jnp.where(iota(weights.shape, 1) < TAPS, 1.0, -1.0)
    both = jnp.concatenate([weights * sign, pltpu.roll(weights, TAPS, 1)], 0)
    clean = total - dot(both, taps)

    inside = iota((blocks, length), 1) // BLOCK == iota((blocks, length), 0)

    def spread(row):
        return jnp.where(inside, jnp.broadcast_to(row, (blocks, length)), 0.0)

    for m in range(beams):
        re, im = clean[m : m + 1], clean[beams + m : beams + m + 1]
        base = 2 * blocks * m
        emb[0, base : base + blocks, :] = spread(re)
        emb[0, base + blocks : base + 2 * blocks, :] = spread(im)
        emb[1, base : base + blocks, :] = spread(im)
        emb[1, base + blocks : base + 2 * blocks, :] = spread(-re)
    lagged = dot_nt(lagt[0], emb[0]) + dot_nt(lagt[1], emb[1])
    own = LAGS // nt
    for dest in range(nt):
        lg[dest] = lagged[own * dest : own * (dest + 1), :]
    tm_start(lg_copy)
    lg_buf[d] = lg[d]
    tm_wait_recv(lg_copy)

    wide = 2 * blocks
    group = 128 // wide
    slot_of = iota((own, 128), 1) // wide
    rows = []
    for m in range(beams):
        pieces = []
        for start in range(0, nt, group):
            acc = jnp.zeros((own, 128), jnp.float32)
            for s in range(group):
                moved = pltpu.roll(lg_buf[start + s], (wide * (s - m)) % 128, 1)
                acc = jnp.where(slot_of == s, moved, acc)
            pieces.append(acc)
        rows.append(jnp.concatenate(pieces, 1))
    spectrum = dot(jnp.concatenate(rows, 0), table_ref[...])
    for m in range(beams):
        for part_id in range(2):
            out_ref[m, part_id] = spectrum[own * m : own * (m + 1), DOPPLER * part_id : DOPPLER * (part_id + 1)]

    tm_wait_send(gm_copy)
    tm_wait_send(xm_copy)
    tm_wait_send(lg_copy)

    def rs_drain(j, _):
        peer = chan_peer(j)
        rs_copy(peer, peer).wait_send()
        return 0

    lax.fori_loop(0, nc - 1, rs_drain, 0)


def doppler_table(blocks_total, blocks):
    q = np.arange(blocks_total)
    angle = 2.0 * np.pi * ((q[:, None] * np.arange(DOPPLER)[None, :]) % DOPPLER) / DOPPLER
    cosine, sine = np.cos(angle), np.sin(angle)
    first = np.concatenate([cosine, -sine], 1).reshape(-1, 1, blocks, 2 * DOPPLER)
    second = np.concatenate([sine, cosine], 1).reshape(-1, 1, blocks, 2 * DOPPLER)
    scale = 0.125 / math.sqrt(blocks_total * BLOCK)
    table = np.concatenate([first, second], 1).reshape(2 * blocks_total, 2 * DOPPLER) * scale
    return table.astype(np.float32)


def on_device(ref_signal, surveillance, steering):
    nc, nt = lax.axis_size("chan"), lax.axis_size("tm")
    length = ref_signal.shape[1]
    chans = surveillance.shape[1]
    beams = steering.shape[1] // nc
    blocks = length // BLOCK
    own = LAGS // nt
    w = steering.reshape(2, nc, beams, chans)
    rows = jnp.stack([jnp.concatenate([w[0], -w[1]], -1), jnp.concatenate([w[1], w[0]], -1)], 1)
    table = jnp.asarray(doppler_table(nt * blocks, blocks))
    vmem = pl.BlockSpec(memory_space=pltpu.VMEM)
    f32 = jnp.float32
    cols = 2 * blocks * beams
    return pl.pallas_call(
        functools.partial(kernel, nc, nt),
        out_shape=jax.ShapeDtypeStruct((beams, 2, own, DOPPLER), f32),
        in_specs=[vmem] * 4,
        out_specs=vmem,
        scratch_shapes=[
            pltpu.VMEM((nc, 2 * beams, length), f32),
            pltpu.VMEM((nc, 2 * beams, length), f32),
            pltpu.VMEM((2, HALO), f32),
            pltpu.VMEM((2, LAGS, length), f32),
            pltpu.VMEM((2, 2 * TAPS), f32),
            pltpu.VMEM((nt, 2, 2 * TAPS), f32),
            pltpu.VMEM((beams, 2 * TAPS), f32),
            pltpu.VMEM((nt, beams, 2 * TAPS), f32),
            pltpu.VMEM((2, 128, length), f32),
            pltpu.VMEM((nt, own, 128), f32),
            pltpu.VMEM((nt, own, 128), f32),
            pltpu.SemaphoreType.DMA,
            pltpu.SemaphoreType.DMA,
            pltpu.SemaphoreType.DMA((nc,)),
            pltpu.SemaphoreType.DMA((nc,)),
            pltpu.SemaphoreType.DMA((nt,)),
            pltpu.SemaphoreType.DMA((nt,)),
            pltpu.SemaphoreType.DMA((nt,)),
            pltpu.SemaphoreType.DMA((nt,)),
            pltpu.SemaphoreType.DMA((nt,)),
            pltpu.SemaphoreType.DMA((nt,)),
        ],
        compiler_params=pltpu.CompilerParams(collective_id=0, has_side_effects=True, vmem_limit_bytes=60 << 20),
        name="radar",
    )(ref_signal, surveillance.reshape(2 * chans, length), rows.reshape(2 * beams * nc, 2 * chans), table)


def solution(mesh):
    placed = (P(None, "tm"), P(None, "chan", "tm"), P(None, None, "chan"))
    return jax.shard_map(
        on_device,
        mesh=mesh,
        in_specs=placed,
        out_specs=P("chan", None, "tm", None),
        check_vma=False,
    )
```

```python
import functools
import math

import jax
import jax.numpy as jnp
import numpy as np
from jax import lax
from jax.experimental import pallas as pl
from jax.experimental.pallas import tpu as pltpu
from jax.sharding import PartitionSpec as P

LAGS = 256
DOPPLER = 256
TAPS = 64
BLOCK = 256
HALO = 256
MESH = pl.DeviceIdType.MESH
HIGHEST = lax.Precision.HIGHEST


def dot(a, b):
    return lax.dot_general(a, b, (((1,), (0,)), ((), ())), precision=HIGHEST, preferred_element_type=jnp.float32)


def dot_nt(a, b):
    return lax.dot_general(a, b, (((1,), (1,)), ((), ())), precision=HIGHEST, preferred_element_type=jnp.float32)


def bdot(a, b):
    return lax.dot_general(a, b, (((1,), (0,)), ((), ())), preferred_element_type=jnp.float32)


def bdot_nt(a, b):
    return lax.dot_general(a, b, (((1,), (1,)), ((), ())), preferred_element_type=jnp.float32)


def split(x, terms):
    out = []
    for _ in range(terms):
        head = x.astype(jnp.bfloat16).astype(jnp.float32)
        out.append(head)
        x = x - head
    return out


def iota(shape, dim):
    return lax.broadcasted_iota(jnp.int32, shape, dim)


def conj_pack(a, b):
    half = a.shape[1] // 2
    sign = jnp.where(iota(a.shape, 1) < half, 1.0, -1.0)
    return sign * a + pltpu.roll(b, half, 1)


def widen(packed):
    half = packed.shape[1] // 2
    sign = jnp.where(iota(packed.shape, 1) < half, 1.0, -1.0)
    return jnp.concatenate([packed * sign, pltpu.roll(packed, half, 1)], 0)


def hermitian_inverse(m):
    n = m.shape[0]
    wide = (n, 2 * n)
    lane = iota((1, 2 * n), 1)
    row_id = iota((n, 1), 0)
    flip = jnp.where(lane < n, -1.0, 1.0)
    for k in range(0, n, 2):
        c0r, c1r, c0i, c1i = (jnp.broadcast_to(m[:, j : j + 1], wide) for j in (k, k + 1, n + k, n + k + 1))
        a, d = c0r[k : k + 1], c1r[k + 1 : k + 2]
        br, bi = c1r[k : k + 1], c1i[k : k + 1]
        inv = 1.0 / (a * d - (br * br + bi * bi))
        at0, at1 = lane == k, lane == k + 1
        here = at0 | at1 | (lane == n + k) | (lane == n + k + 1)
        r0 = jnp.where(here, jnp.where(at0, 1.0, 0.0), m[k : k + 1])
        r1 = jnp.where(here, jnp.where(at1, 1.0, 0.0), m[k + 1 : k + 2])
        t0 = pltpu.roll(r0, n, 1) * flip
        t1 = pltpu.roll(r1, n, 1) * flip
        a, d, br, bi = a * inv, d * inv, br * inv, bi * inv
        n0 = d * r0 - br * r1 - bi * t1
        u0 = d * t0 - br * t1 + bi * r1
        n1 = a * r1 - br * r0 + bi * t0
        u1 = a * t1 - br * t0 - bi * r0
        rest = (jnp.where(here, 0.0, m) - c0r * n0 - c1r * n1) - (c0i * u0 + c1i * u1)
        m = jnp.where(row_id == k, n0, jnp.where(row_id == k + 1, n1, rest))
    return m


def gram_matrix(g_row, e_row):
    n = TAPS
    row = iota((n, 2 * n), 0)
    lane = iota((n, 2 * n), 1)
    col = lane % n
    sign = jnp.where(lane < n, 1.0, -1.0)

    def shifted(v):
        return pltpu.roll(jnp.broadcast_to(v, (n, 2 * n)), 0, 1, stride=1, stride_axis=0)

    upper = jnp.where(col >= row, shifted(g_row), 0.0)
    flipped = jnp.concatenate([upper, jnp.zeros_like(upper)], 0).T
    lower = flipped[:n] - pltpu.roll(flipped[n:], n, 1)
    toeplitz = jnp.where(col >= row, upper, lower)
    tail = jnp.where((col >= row) & (row >= 1), shifted(e_row), 0.0)
    tail = jnp.concatenate([tail, jnp.zeros_like(tail)], 0)
    square = dot(tail.T, tail)
    return toeplitz - (square[:n] + sign * pltpu.roll(square[n:], n, 1))


def kernel(nc, nt, ref_ref, surv_ref, w_ref, table_ref, out_ref,
           part, core_buf, chip_send, chip_buf, halo, lagt, lag_hi, lag_mid, tap_lo, gm, gm_buf, xm, xm_buf, emb, lg, lg_buf,
           halo_ss, halo_rs, core_ss, core_rs, rs_ss, rs_rs, gm_ss, gm_rs, xm_ss, xm_rs, lg_ss, lg_rs):
    c = lax.axis_index("chan")
    d = lax.axis_index("tm")
    length = ref_ref.shape[1]
    beams = part.shape[2] // 2
    chips = nc // 2
    core, chip = c % 2, c // 2
    partner = c + 1 - 2 * core
    blocks = length // BLOCK

    def tm_peer(j):
        return lax.rem(d + nt // 2 + (1 - 2 * (j % 2)) * ((j + 1) // 2) + nt, nt)

    def chan_peer(j):
        return lax.rem(c + 1 + j, nc)

    barrier = pltpu.get_barrier_semaphore()

    def greet_chan(j, _):
        pl.semaphore_signal(barrier, inc=1, device_id={"chan": chan_peer(j)}, device_id_type=MESH)
        return 0

    def greet_tm(j, _):
        pl.semaphore_signal(barrier, inc=1, device_id={"tm": tm_peer(j)}, device_id_type=MESH)
        return 0

    lax.fori_loop(0, nt - 1, greet_tm, 0)
    lax.fori_loop(0, nc - 1, greet_chan, 0)

    w_re, w_im = w_ref[0], w_ref[1]
    survey = jnp.concatenate([surv_ref[0], surv_ref[1]], 0)
    part_re = dot(jnp.concatenate([w_re, -w_im], 1), survey)
    part_im = dot(jnp.concatenate([w_im, w_re], 1), survey)
    for owner in range(nc):
        rows = slice(beams * owner, beams * (owner + 1))
        part[owner % 2, owner // 2] = jnp.concatenate([part_re[rows], part_im[rows]], 0)

    pl.semaphore_wait(barrier, nt - 1 + nc - 1)

    right = lax.rem(d + 1, nt)
    halo_copy = pltpu.make_async_remote_copy(
        src_ref=ref_ref.at[:, pl.ds(length - HALO, HALO)], dst_ref=halo, send_sem=halo_ss, recv_sem=halo_rs,
        device_id={"tm": right}, device_id_type=MESH)
    halo_copy.start()

    def chip_peer(j):
        return lax.rem(chip + 1 + j, chips)

    def core_copy(j):
        return pltpu.make_async_remote_copy(
            src_ref=part.at[1 - core, j], dst_ref=core_buf.at[j], send_sem=core_ss.at[j], recv_sem=core_rs.at[j],
            device_id={"chan": partner}, device_id_type=MESH)

    def rs_copy(peer, slot):
        return pltpu.make_async_remote_copy(
            src_ref=chip_send.at[peer], dst_ref=chip_buf.at[slot], send_sem=rs_ss.at[peer], recv_sem=rs_rs.at[slot],
            device_id={"chan": 2 * peer + core}, device_id_type=MESH)

    def core_start(j, _):
        core_copy(chip_peer(j)).start()
        return 0

    lax.fori_loop(0, chips, core_start, 0)

    def rs_start(j, _):
        peer = chip_peer(j)
        core_copy(peer).wait_recv()
        chip_send[peer] = part[core, peer] + core_buf[peer]
        rs_copy(peer, chip).start()
        return 0

    lax.fori_loop(0, chips - 1, rs_start, 0)
    core_copy(chip).wait_recv()
    chip_buf[chip] = part[core, chip] + core_buf[chip]

    halo_copy.wait()
    ref = ref_ref[...]
    before = jnp.where(d == 0, 0.0, halo[...])
    extended = jnp.concatenate([before, ref], 1)
    for p in range(2):
        shifted = pltpu.roll(
            jnp.broadcast_to(extended[p : p + 1, :], (LAGS, HALO + length)), 0, 1, stride=1, stride_axis=0)
        lagt[p] = shifted[:, HALO:]
    taps = jnp.concatenate([lagt[0, :TAPS, :], lagt[1, :TAPS, :]], 0)

    row8 = iota((8, length), 0)
    mark = jnp.where((iota((8, length), 1) == length - 1) & (d == nt - 1), 1.0, 0.0)
    probe = jnp.where(row8 == 0, ref[0:1], jnp.where(row8 == 1, ref[1:2], jnp.where(row8 == 2, mark, 0.0)))
    g_raw = dot_nt(probe, taps)
    g_conj = conj_pack(g_raw[0:1], g_raw[1:2])
    gm[0:1, :] = jnp.where(iota(g_conj.shape, 1) < TAPS, g_conj, -g_conj)
    gm[1:2, :] = g_raw[2:3]

    def gm_copy(peer, slot):
        return pltpu.make_async_remote_copy(
            src_ref=gm, dst_ref=gm_buf.at[slot], send_sem=gm_ss.at[peer], recv_sem=gm_rs.at[slot],
            device_id={"tm": peer}, device_id_type=MESH)

    def xm_copy(peer, slot):
        return pltpu.make_async_remote_copy(
            src_ref=xm, dst_ref=xm_buf.at[slot], send_sem=xm_ss.at[peer], recv_sem=xm_rs.at[slot],
            device_id={"tm": peer}, device_id_type=MESH)

    def lg_copy(peer, slot):
        return pltpu.make_async_remote_copy(
            src_ref=lg.at[peer], dst_ref=lg_buf.at[slot], send_sem=lg_ss.at[peer], recv_sem=lg_rs.at[slot],
            device_id={"tm": peer}, device_id_type=MESH)

    def tm_start(copy):
        def body(j, _):
            copy(tm_peer(j), d).start()
            return 0

        lax.fori_loop(0, nt - 1, body, 0)

    def tm_wait_recv(copy):
        def body(j, _):
            peer = tm_peer(j)
            copy(peer, peer).wait_recv()
            return 0

        lax.fori_loop(0, nt - 1, body, 0)

    def tm_wait_send(copy):
        def body(j, _):
            peer = tm_peer(j)
            copy(peer, peer).wait_send()
            return 0

        lax.fori_loop(0, nt - 1, body, 0)

    tm_start(gm_copy)
    gm_buf[d] = gm[...]

    for p in range(2):
        hi, mid, lo = split(lagt[p], 3)
        lag_hi[LAGS * p : LAGS * (p + 1)] = hi.astype(jnp.bfloat16)
        lag_mid[LAGS * p : LAGS * (p + 1)] = mid.astype(jnp.bfloat16)
        tap_lo[TAPS * p : TAPS * (p + 1)] = lo[:TAPS].astype(jnp.bfloat16)
    tap_terms = [jnp.concatenate([lag_hi[:TAPS], lag_hi[LAGS : LAGS + TAPS]], 0),
                 jnp.concatenate([lag_mid[:TAPS], lag_mid[LAGS : LAGS + TAPS]], 0), tap_lo[...]]

    def rs_wait(j, _):
        peer = chip_peer(j)
        rs_copy(peer, peer).wait_recv()
        return 0

    lax.fori_loop(0, chips - 1, rs_wait, 0)
    total = chip_buf[0]
    for source in range(1, chips):
        total = total + chip_buf[source]

    total_terms = jnp.concatenate(split(total, 3), 0).astype(jnp.bfloat16)
    x_cols = sum(bdot_nt(term, total_terms) for term in tap_terms)
    x_rows = jnp.concatenate([x_cols, jnp.zeros((2 * TAPS, 128 - x_cols.shape[1]), jnp.float32)], 1).T
    x_raw = x_rows[: 2 * beams] + x_rows[2 * beams : 4 * beams] + x_rows[4 * beams : 6 * beams]
    xm[...] = conj_pack(x_raw[:beams], x_raw[beams:])
    tm_start(xm_copy)
    xm_buf[d] = xm[...]

    tm_wait_recv(gm_copy)
    g_sum = jnp.sum(gm_buf[...], axis=0)
    gram = gram_matrix(g_sum[0:1], g_sum[1:2])
    level = 1.0 / gram[0:1, 0:1]
    gram = gram * level
    inverse = widen(hermitian_inverse(gram))
    gram_wide = widen(gram)

    tm_wait_recv(xm_copy)
    x = jnp.sum(xm_buf[...], axis=0) * level
    weights = dot(x, inverse)
    weights = weights + dot(x - dot(weights, gram_wide), inverse)

    sign = jnp.where(iota(weights.shape, 1) < TAPS, 1.0, -1.0)
    both = jnp.concatenate([weights * sign, pltpu.roll(weights, TAPS, 1)], 0)
    both_terms = jnp.concatenate(split(both, 3), 0).astype(jnp.bfloat16)
    model = sum(bdot(both_terms, term) for term in tap_terms)
    clean = total - (model[: 2 * beams] + model[2 * beams : 4 * beams] + model[4 * beams : 6 * beams])

    inside = iota((blocks, length), 1) // BLOCK == iota((blocks, length), 0)
    cols = 2 * blocks * beams

    def spread(row):
        return jnp.where(inside, jnp.broadcast_to(row, (blocks, length)), 0.0)

    for order, term in enumerate(split(clean, 2)):
        for m in range(beams):
            base = cols * order + 2 * blocks * m
            pair = jnp.concatenate([spread(term[m : m + 1]), spread(term[beams + m : beams + m + 1])], 0)
            emb[base : base + 2 * blocks, :] = pair.astype(jnp.bfloat16)
    products = bdot_nt(lag_hi[...], emb[...]) + bdot_nt(lag_mid[...], emb[...])
    products = products + pltpu.roll(products, cols, 1)
    with_re, with_im = products[:LAGS], products[LAGS:]
    real_lane = iota((LAGS, 2 * cols), 1) % (2 * blocks) < blocks
    lagged = with_re + jnp.where(
        real_lane, pltpu.roll(with_im, 2 * cols - blocks, 1), -pltpu.roll(with_im, blocks, 1))
    own = LAGS // nt
    for dest in range(nt):
        lg[dest] = lagged[own * dest : own * (dest + 1), :]
    tm_start(lg_copy)
    lg_buf[d] = lg[d]
    tm_wait_recv(lg_copy)

    wide = 2 * blocks
    group = 128 // wide
    slot_of = iota((own, 128), 1) // wide
    rows = []
    for m in range(beams):
        pieces = []
        for start in range(0, nt, group):
            acc = jnp.zeros((own, 128), jnp.float32)
            for s in range(group):
                moved = pltpu.roll(lg_buf[start + s], (wide * (s - m)) % 128, 1)
                acc = jnp.where(slot_of == s, moved, acc)
            pieces.append(acc)
        rows.append(jnp.concatenate(pieces, 1))
    stacked = jnp.concatenate(rows, 0)
    height = own * beams
    stacked_terms = jnp.concatenate(split(stacked, 2), 0).astype(jnp.bfloat16)
    spectrum = bdot(stacked_terms, table_ref[0]) + bdot(stacked_terms, table_ref[1])
    spectrum = spectrum[:height] + spectrum[height:]
    for m in range(beams):
        for part_id in range(2):
            out_ref[m, part_id] = spectrum[own * m : own * (m + 1), DOPPLER * part_id : DOPPLER * (part_id + 1)]

    tm_wait_send(gm_copy)
    tm_wait_send(xm_copy)
    tm_wait_send(lg_copy)

    def rs_drain(j, _):
        peer = chip_peer(j)
        rs_copy(peer, peer).wait_send()
        return 0

    def core_drain(j, _):
        core_copy(j).wait_send()
        return 0

    lax.fori_loop(0, chips - 1, rs_drain, 0)
    lax.fori_loop(0, chips, core_drain, 0)


def doppler_table(blocks_total, blocks):
    q = np.arange(blocks_total)
    angle = 2.0 * np.pi * ((q[:, None] * np.arange(DOPPLER)[None, :]) % DOPPLER) / DOPPLER
    cosine, sine = np.cos(angle), np.sin(angle)
    first = np.concatenate([cosine, -sine], 1).reshape(-1, 1, blocks, 2 * DOPPLER)
    second = np.concatenate([sine, cosine], 1).reshape(-1, 1, blocks, 2 * DOPPLER)
    scale = 0.125 / math.sqrt(blocks_total * BLOCK)
    table = np.concatenate([first, second], 1).reshape(2 * blocks_total, 2 * DOPPLER) * scale
    head = table.astype(np.float32).astype(jnp.bfloat16)
    tail = (table - head.astype(np.float64)).astype(np.float32).astype(jnp.bfloat16)
    return np.stack([head, tail])


def on_device(ref_signal, surveillance, steering):
    nc, nt = lax.axis_size("chan"), lax.axis_size("tm")
    length = ref_signal.shape[1]
    chans = surveillance.shape[1]
    beams = steering.shape[1] // nc
    blocks = length // BLOCK
    own = LAGS // nt
    table = jnp.asarray(doppler_table(nt * blocks, blocks))
    vmem = pl.BlockSpec(memory_space=pltpu.VMEM)
    f32, bf16 = jnp.float32, jnp.bfloat16
    chips = nc // 2
    return pl.pallas_call(
        functools.partial(kernel, nc, nt),
        out_shape=jax.ShapeDtypeStruct((beams, 2, own, DOPPLER), f32),
        in_specs=[vmem] * 4,
        out_specs=vmem,
        scratch_shapes=[
            pltpu.VMEM((2, chips, 2 * beams, length), f32),
            pltpu.VMEM((chips, 2 * beams, length), f32),
            pltpu.VMEM((chips, 2 * beams, length), f32),
            pltpu.VMEM((chips, 2 * beams, length), f32),
            pltpu.VMEM((2, HALO), f32),
            pltpu.VMEM((2, LAGS, length), f32),
            pltpu.VMEM((2 * LAGS, length), bf16),
            pltpu.VMEM((2 * LAGS, length), bf16),
            pltpu.VMEM((2 * TAPS, length), bf16),
            pltpu.VMEM((2, 2 * TAPS), f32),
            pltpu.VMEM((nt, 2, 2 * TAPS), f32),
            pltpu.VMEM((beams, 2 * TAPS), f32),
            pltpu.VMEM((nt, beams, 2 * TAPS), f32),
            pltpu.VMEM((4 * blocks * beams, length), bf16),
            pltpu.VMEM((nt, own, 128), f32),
            pltpu.VMEM((nt, own, 128), f32),
            pltpu.SemaphoreType.DMA,
            pltpu.SemaphoreType.DMA,
            pltpu.SemaphoreType.DMA((chips,)),
            pltpu.SemaphoreType.DMA((chips,)),
            pltpu.SemaphoreType.DMA((chips,)),
            pltpu.SemaphoreType.DMA((chips,)),
            pltpu.SemaphoreType.DMA((nt,)),
            pltpu.SemaphoreType.DMA((nt,)),
            pltpu.SemaphoreType.DMA((nt,)),
            pltpu.SemaphoreType.DMA((nt,)),
            pltpu.SemaphoreType.DMA((nt,)),
            pltpu.SemaphoreType.DMA((nt,)),
        ],
        compiler_params=pltpu.CompilerParams(collective_id=0, has_side_effects=True, vmem_limit_bytes=60 << 20),
        name="radar",
    )(ref_signal, surveillance, steering, table)


def solution(mesh):
    placed = (P(None, "tm"), P(None, "chan", "tm"), P(None, None, "chan"))
    return jax.shard_map(
        on_device,
        mesh=mesh,
        in_specs=placed,
        out_specs=P("chan", None, "tm", None),
        check_vma=False,
    )
```

```python
import functools
import math

import jax
import jax.numpy as jnp
import numpy as np
from jax import lax
from jax.experimental import pallas as pl
from jax.experimental.pallas import tpu as pltpu
from jax.sharding import PartitionSpec as P

LAGS = 256
DOPPLER = 256
TAPS = 64
BLOCK = 256
HALO = 256
MESH = pl.DeviceIdType.MESH
HIGHEST = lax.Precision.HIGHEST


def dot(a, b):
    return lax.dot_general(a, b, (((1,), (0,)), ((), ())), precision=HIGHEST, preferred_element_type=jnp.float32)


def dot_nt(a, b):
    return lax.dot_general(a, b, (((1,), (1,)), ((), ())), precision=HIGHEST, preferred_element_type=jnp.float32)


def bdot(a, b):
    return lax.dot_general(a, b, (((1,), (0,)), ((), ())), preferred_element_type=jnp.float32)


def bdot_nt(a, b):
    return lax.dot_general(a, b, (((1,), (1,)), ((), ())), preferred_element_type=jnp.float32)


def split(x, terms):
    out = []
    for _ in range(terms):
        head = x.astype(jnp.bfloat16).astype(jnp.float32)
        out.append(head)
        x = x - head
    return out


def iota(shape, dim):
    return lax.broadcasted_iota(jnp.int32, shape, dim)


def conj_pack(a, b):
    half = a.shape[1] // 2
    sign = jnp.where(iota(a.shape, 1) < half, 1.0, -1.0)
    return sign * a + pltpu.roll(b, half, 1)


def widen(packed):
    half = packed.shape[1] // 2
    sign = jnp.where(iota(packed.shape, 1) < half, 1.0, -1.0)
    return jnp.concatenate([packed * sign, pltpu.roll(packed, half, 1)], 0)


def hermitian_inverse(m):
    n = m.shape[0]
    wide = (n, 2 * n)
    lane = iota((1, 2 * n), 1)
    row_id = iota((n, 1), 0)
    flip = jnp.where(lane < n, -1.0, 1.0)
    for k in range(0, n, 2):
        c0r, c1r, c0i, c1i = (jnp.broadcast_to(m[:, j : j + 1], wide) for j in (k, k + 1, n + k, n + k + 1))
        a, d = c0r[k : k + 1], c1r[k + 1 : k + 2]
        br, bi = c1r[k : k + 1], c1i[k : k + 1]
        inv = 1.0 / (a * d - (br * br + bi * bi))
        at0, at1 = lane == k, lane == k + 1
        here = at0 | at1 | (lane == n + k) | (lane == n + k + 1)
        r0 = jnp.where(here, jnp.where(at0, 1.0, 0.0), m[k : k + 1])
        r1 = jnp.where(here, jnp.where(at1, 1.0, 0.0), m[k + 1 : k + 2])
        t0 = pltpu.roll(r0, n, 1) * flip
        t1 = pltpu.roll(r1, n, 1) * flip
        a, d, br, bi = a * inv, d * inv, br * inv, bi * inv
        n0 = d * r0 - br * r1 - bi * t1
        u0 = d * t0 - br * t1 + bi * r1
        n1 = a * r1 - br * r0 + bi * t0
        u1 = a * t1 - br * t0 - bi * r0
        rest = (jnp.where(here, 0.0, m) - c0r * n0 - c1r * n1) - (c0i * u0 + c1i * u1)
        m = jnp.where(row_id == k, n0, jnp.where(row_id == k + 1, n1, rest))
    return m


def gram_matrix(g_row, e_row):
    n = TAPS
    row = iota((n, 2 * n), 0)
    lane = iota((n, 2 * n), 1)
    col = lane % n
    sign = jnp.where(lane < n, 1.0, -1.0)

    def shifted(v):
        return pltpu.roll(jnp.broadcast_to(v, (n, 2 * n)), 0, 1, stride=1, stride_axis=0)

    upper = jnp.where(col >= row, shifted(g_row), 0.0)
    flipped = jnp.concatenate([upper, jnp.zeros_like(upper)], 0).T
    lower = flipped[:n] - pltpu.roll(flipped[n:], n, 1)
    toeplitz = jnp.where(col >= row, upper, lower)
    tail = jnp.where((col >= row) & (row >= 1), shifted(e_row), 0.0)
    tail = jnp.concatenate([tail, jnp.zeros_like(tail)], 0)
    square = dot(tail.T, tail)
    return toeplitz - (square[:n] + sign * pltpu.roll(square[n:], n, 1))


def kernel(nc, nt, ref_ref, surv_ref, w_ref, table_ref, out_ref,
           part, core_buf, chip_send, chip_buf, halo, lag_hi, lag_mid, tap_lo, gm, gm_buf, xm, xm_buf, emb, lg, lg_buf,
           reach, halo_ss, halo_rs, core_ss, core_rs, rs_ss, rs_rs, gm_ss, gm_rs, xm_ss, xm_rs, lg_ss, lg_rs):
    c = lax.axis_index("chan")
    d = lax.axis_index("tm")
    length = ref_ref.shape[1]
    beams = part.shape[2] // 2
    chips = nc // 2
    core, chip = c % 2, c // 2
    partner = c + 1 - 2 * core
    blocks = length // BLOCK

    def tm_peer(j):
        return lax.rem(d + nt // 2 + (1 - 2 * (j % 2)) * ((j + 1) // 2) + nt, nt)

    def chan_peer(j):
        return lax.rem(c + 1 + j, nc)

    barrier = pltpu.get_barrier_semaphore()

    def greet_chan(j, _):
        pl.semaphore_signal(barrier, inc=1, device_id={"chan": chan_peer(j)}, device_id_type=MESH)
        return 0

    def tm_near(offset):
        return {"tm": lax.rem(d + offset + nt, nt)}

    lax.fori_loop(0, nc - 1, greet_chan, 0)
    for offset in (-2, -1, 1, 2):
        pl.semaphore_signal(barrier, inc=1, device_id=tm_near(offset), device_id_type=MESH)

    def reach_signal(i):
        for offset in (-(2 << i), 2 << i):
            pl.semaphore_signal(reach.at[i], inc=1, device_id=tm_near(offset), device_id_type=MESH)

    def reach_wait(i):
        pl.semaphore_wait(reach.at[i], 2)

    w_re, w_im = w_ref[0], w_ref[1]
    survey = jnp.concatenate([surv_ref[0], surv_ref[1]], 0)
    part_re = dot(jnp.concatenate([w_re, -w_im], 1), survey)
    part_im = dot(jnp.concatenate([w_im, w_re], 1), survey)
    for owner in range(nc):
        rows = slice(beams * owner, beams * (owner + 1))
        part[owner % 2, owner // 2] = jnp.concatenate([part_re[rows], part_im[rows]], 0)

    pl.semaphore_wait(barrier, nc - 1 + 4)
    reach_signal(0)

    right = lax.rem(d + 1, nt)
    halo_copy = pltpu.make_async_remote_copy(
        src_ref=ref_ref.at[:, pl.ds(length - HALO, HALO)], dst_ref=halo, send_sem=halo_ss, recv_sem=halo_rs,
        device_id={"tm": right}, device_id_type=MESH)
    halo_copy.start()

    def chip_peer(j):
        return lax.rem(chip + 1 + j, chips)

    def core_copy(j):
        return pltpu.make_async_remote_copy(
            src_ref=part.at[1 - core, j], dst_ref=core_buf.at[j], send_sem=core_ss.at[j], recv_sem=core_rs.at[j],
            device_id={"chan": partner}, device_id_type=MESH)

    def rs_copy(peer, slot):
        return pltpu.make_async_remote_copy(
            src_ref=chip_send.at[peer], dst_ref=chip_buf.at[slot], send_sem=rs_ss.at[peer], recv_sem=rs_rs.at[slot],
            device_id={"chan": 2 * peer + core}, device_id_type=MESH)

    def core_start(j, _):
        core_copy(chip_peer(j)).start()
        return 0

    lax.fori_loop(0, chips, core_start, 0)

    def rs_start(j, _):
        peer = chip_peer(j)
        core_copy(peer).wait_recv()
        chip_send[peer] = part[core, peer] + core_buf[peer]
        rs_copy(peer, chip).start()
        return 0

    lax.fori_loop(0, chips - 1, rs_start, 0)
    core_copy(chip).wait_recv()
    chip_buf[chip] = part[core, chip] + core_buf[chip]

    reach_wait(0)
    reach_signal(1)

    halo_copy.wait()
    ref = ref_ref[...]
    before = jnp.where(d == 0, 0.0, halo[...])
    extended = jnp.concatenate([before, ref], 1)

    def lags_of(p, first, count):
        row = jnp.broadcast_to(extended[p : p + 1, :], (count, HALO + length))
        return pltpu.roll(row, first, 1, stride=1, stride_axis=0)[:, HALO:]

    taps = jnp.concatenate([lags_of(0, 0, TAPS), lags_of(1, 0, TAPS)], 0)
    taps_hi, taps_mid, taps_lo = split(taps, 3)
    for p in range(2):
        lag_hi[LAGS * p : LAGS * p + TAPS] = taps_hi[TAPS * p : TAPS * (p + 1)].astype(jnp.bfloat16)
        lag_mid[LAGS * p : LAGS * p + TAPS] = taps_mid[TAPS * p : TAPS * (p + 1)].astype(jnp.bfloat16)
    tap_lo[...] = taps_lo.astype(jnp.bfloat16)
    reach_wait(1)
    reach_signal(2)
    tap_terms = [jnp.concatenate([lag_hi[:TAPS], lag_hi[LAGS : LAGS + TAPS]], 0),
                 jnp.concatenate([lag_mid[:TAPS], lag_mid[LAGS : LAGS + TAPS]], 0), tap_lo[...]]

    def lag_products(rows8):
        terms = jnp.concatenate(split(rows8, 3), 0).astype(jnp.bfloat16)
        cols = sum(bdot_nt(term, terms) for term in tap_terms)
        turned = jnp.concatenate([cols, jnp.zeros((2 * TAPS, 128 - cols.shape[1]), jnp.float32)], 1).T
        return turned[:8] + turned[8:16] + turned[16:24]

    row8 = iota((8, length), 0)
    mark = jnp.where((iota((8, length), 1) == length - 1) & (d == nt - 1), 1.0, 0.0)
    probe = jnp.where(row8 == 0, ref[0:1], jnp.where(row8 == 1, ref[1:2], jnp.where(row8 == 2, mark, 0.0)))
    g_raw = lag_products(probe)
    g_conj = conj_pack(g_raw[0:1], g_raw[1:2])
    gm[0:1, :] = jnp.where(iota(g_conj.shape, 1) < TAPS, g_conj, -g_conj)
    gm[1:2, :] = g_raw[2:3]

    def gm_copy(peer, slot):
        return pltpu.make_async_remote_copy(
            src_ref=gm, dst_ref=gm_buf.at[slot], send_sem=gm_ss.at[peer], recv_sem=gm_rs.at[slot],
            device_id={"tm": peer}, device_id_type=MESH)

    def xm_copy(peer, slot):
        return pltpu.make_async_remote_copy(
            src_ref=xm, dst_ref=xm_buf.at[slot], send_sem=xm_ss.at[peer], recv_sem=xm_rs.at[slot],
            device_id={"tm": peer}, device_id_type=MESH)

    def lg_copy(peer, slot):
        return pltpu.make_async_remote_copy(
            src_ref=lg.at[peer], dst_ref=lg_buf.at[slot], send_sem=lg_ss.at[peer], recv_sem=lg_rs.at[slot],
            device_id={"tm": peer}, device_id_type=MESH)

    def tm_start(copy):
        def body(j, _):
            copy(tm_peer(j), d).start()
            return 0

        lax.fori_loop(0, nt - 1, body, 0)

    def tm_wait_recv(copy):
        def body(j, _):
            peer = tm_peer(j)
            copy(peer, peer).wait_recv()
            return 0

        lax.fori_loop(0, nt - 1, body, 0)

    def tm_wait_send(copy):
        def body(j, _):
            peer = tm_peer(j)
            copy(peer, peer).wait_send()
            return 0

        lax.fori_loop(0, nt - 1, body, 0)

    reach_wait(2)
    tm_start(gm_copy)
    gm_buf[d] = gm[...]

    for p in range(2):
        hi, mid = split(lags_of(p, TAPS, LAGS - TAPS), 2)
        lag_hi[LAGS * p + TAPS : LAGS * (p + 1)] = hi.astype(jnp.bfloat16)
        lag_mid[LAGS * p + TAPS : LAGS * (p + 1)] = mid.astype(jnp.bfloat16)

    def rs_wait(j, _):
        peer = chip_peer(j)
        rs_copy(peer, peer).wait_recv()
        return 0

    lax.fori_loop(0, chips - 1, rs_wait, 0)
    total = chip_buf[0]
    for source in range(1, chips):
        total = total + chip_buf[source]

    x_raw = lag_products(total)
    xm[...] = conj_pack(x_raw[:beams], x_raw[beams:])
    tm_start(xm_copy)
    xm_buf[d] = xm[...]

    tm_wait_recv(gm_copy)
    g_sum = jnp.sum(gm_buf[...], axis=0)
    gram = gram_matrix(g_sum[0:1], g_sum[1:2])
    level = 1.0 / gram[0:1, 0:1]
    gram = gram * level
    inverse = widen(hermitian_inverse(gram))
    gram_wide = widen(gram)

    tm_wait_recv(xm_copy)
    x = jnp.sum(xm_buf[...], axis=0) * level
    weights = dot(x, inverse)
    weights = weights + dot(x - dot(weights, gram_wide), inverse)

    sign = jnp.where(iota(weights.shape, 1) < TAPS, 1.0, -1.0)
    both = jnp.concatenate([weights * sign, pltpu.roll(weights, TAPS, 1)], 0)
    both_terms = jnp.concatenate(split(both, 3), 0).astype(jnp.bfloat16)
    model = sum(bdot(both_terms, term) for term in tap_terms)
    clean = total - (model[: 2 * beams] + model[2 * beams : 4 * beams] + model[4 * beams : 6 * beams])

    inside = iota((blocks, length), 1) // BLOCK == iota((blocks, length), 0)
    cols = 2 * blocks * beams

    def spread(row):
        return jnp.where(inside, jnp.broadcast_to(row, (blocks, length)), 0.0)

    for order, term in enumerate(split(clean, 2)):
        for m in range(beams):
            base = cols * order + 2 * blocks * m
            pair = jnp.concatenate([spread(term[m : m + 1]), spread(term[beams + m : beams + m + 1])], 0)
            emb[base : base + 2 * blocks, :] = pair.astype(jnp.bfloat16)
    own = LAGS // nt
    half = own // 2
    groups = 4
    span = LAGS // groups
    targets = nt // groups
    real_lane = iota((span, 2 * cols), 1) % (2 * blocks) < blocks
    low_lane = iota((half, 2 * cols), 1) < cols

    def correlate(step, _):
        group = lax.rem(d // targets + groups // 2 + step, groups)

        def both_terms_of(p):
            rows = pl.ds(pl.multiple_of(LAGS * p + span * group, span), span)
            sums = bdot_nt(lag_hi[rows, :], emb[...]) + bdot_nt(lag_mid[rows, :], emb[...])
            return sums + pltpu.roll(sums, cols, 1)

        with_re, with_im = both_terms_of(0), both_terms_of(1)
        lagged = with_re + jnp.where(
            real_lane, pltpu.roll(with_im, 2 * cols - blocks, 1), -pltpu.roll(with_im, blocks, 1))
        for i in range(targets):
            lg[targets * group + i] = jnp.where(
                low_lane, lagged[own * i : own * i + half], lagged[own * i + half : own * (i + 1)])

        def send(i, _):
            peer = targets * group + i

            @pl.when(peer != d)
            def _():
                lg_copy(peer, d).start()

            return 0

        lax.fori_loop(0, targets, send, 0)
        return 0

    lax.fori_loop(0, groups, correlate, 0)
    lg_buf[d] = lg[d]
    tm_wait_recv(lg_copy)

    wide = 2 * blocks
    group = 128 // wide
    slot_of = iota((own, 128), 1) // wide
    upper_row = iota((own, 128), 0) < half

    def received(s):
        twice = jnp.concatenate([lg_buf[s], lg_buf[s]], 0)
        return jnp.where(upper_row, twice, pltpu.roll(twice, 64, 1))

    arrived = [received(s) for s in range(nt)]
    rows = []
    for m in range(beams):
        pieces = []
        for start in range(0, nt, group):
            acc = jnp.zeros((own, 128), jnp.float32)
            for s in range(group):
                moved = pltpu.roll(arrived[start + s], (wide * (s - m)) % 128, 1)
                acc = jnp.where(slot_of == s, moved, acc)
            pieces.append(acc)
        rows.append(jnp.concatenate(pieces, 1))
    stacked = jnp.concatenate(rows, 0)
    height = own * beams
    stacked_terms = jnp.concatenate(split(stacked, 2), 0).astype(jnp.bfloat16)
    spectrum = bdot(stacked_terms, table_ref[0]) + bdot(stacked_terms, table_ref[1])
    spectrum = spectrum[:height] + spectrum[height:]
    for m in range(beams):
        for part_id in range(2):
            out_ref[m, part_id] = spectrum[own * m : own * (m + 1), DOPPLER * part_id : DOPPLER * (part_id + 1)]

    tm_wait_send(gm_copy)
    tm_wait_send(xm_copy)
    tm_wait_send(lg_copy)

    def rs_drain(j, _):
        peer = chip_peer(j)
        rs_copy(peer, peer).wait_send()
        return 0

    def core_drain(j, _):
        core_copy(j).wait_send()
        return 0

    lax.fori_loop(0, chips - 1, rs_drain, 0)
    lax.fori_loop(0, chips, core_drain, 0)


def doppler_table(blocks_total, blocks):
    q = np.arange(blocks_total)
    angle = 2.0 * np.pi * ((q[:, None] * np.arange(DOPPLER)[None, :]) % DOPPLER) / DOPPLER
    cosine, sine = np.cos(angle), np.sin(angle)
    first = np.concatenate([cosine, -sine], 1).reshape(-1, 1, blocks, 2 * DOPPLER)
    second = np.concatenate([sine, cosine], 1).reshape(-1, 1, blocks, 2 * DOPPLER)
    scale = 0.125 / math.sqrt(blocks_total * BLOCK)
    table = np.concatenate([first, second], 1).reshape(2 * blocks_total, 2 * DOPPLER) * scale
    head = table.astype(np.float32).astype(jnp.bfloat16)
    tail = (table - head.astype(np.float64)).astype(np.float32).astype(jnp.bfloat16)
    return np.stack([head, tail])


def on_device(ref_signal, surveillance, steering):
    nc, nt = lax.axis_size("chan"), lax.axis_size("tm")
    length = ref_signal.shape[1]
    chans = surveillance.shape[1]
    beams = steering.shape[1] // nc
    blocks = length // BLOCK
    own = LAGS // nt
    table = jnp.asarray(doppler_table(nt * blocks, blocks))
    vmem = pl.BlockSpec(memory_space=pltpu.VMEM)
    f32, bf16 = jnp.float32, jnp.bfloat16
    chips = nc // 2
    return pl.pallas_call(
        functools.partial(kernel, nc, nt),
        out_shape=jax.ShapeDtypeStruct((beams, 2, own, DOPPLER), f32),
        in_specs=[vmem] * 4,
        out_specs=vmem,
        scratch_shapes=[
            pltpu.VMEM((2, chips, 2 * beams, length), f32),
            pltpu.VMEM((chips, 2 * beams, length), f32),
            pltpu.VMEM((chips, 2 * beams, length), f32),
            pltpu.VMEM((chips, 2 * beams, length), f32),
            pltpu.VMEM((2, HALO), f32),
            pltpu.VMEM((2 * LAGS, length), bf16),
            pltpu.VMEM((2 * LAGS, length), bf16),
            pltpu.VMEM((2 * TAPS, length), bf16),
            pltpu.VMEM((2, 2 * TAPS), f32),
            pltpu.VMEM((nt, 2, 2 * TAPS), f32),
            pltpu.VMEM((beams, 2 * TAPS), f32),
            pltpu.VMEM((nt, beams, 2 * TAPS), f32),
            pltpu.VMEM((4 * blocks * beams, length), bf16),
            pltpu.VMEM((nt, own // 2, 128), f32),
            pltpu.VMEM((nt, own // 2, 128), f32),
            pltpu.SemaphoreType.REGULAR((3,)),
            pltpu.SemaphoreType.DMA,
            pltpu.SemaphoreType.DMA,
            pltpu.SemaphoreType.DMA((chips,)),
            pltpu.SemaphoreType.DMA((chips,)),
            pltpu.SemaphoreType.DMA((chips,)),
            pltpu.SemaphoreType.DMA((chips,)),
            pltpu.SemaphoreType.DMA((nt,)),
            pltpu.SemaphoreType.DMA((nt,)),
            pltpu.SemaphoreType.DMA((nt,)),
            pltpu.SemaphoreType.DMA((nt,)),
            pltpu.SemaphoreType.DMA((nt,)),
            pltpu.SemaphoreType.DMA((nt,)),
        ],
        compiler_params=pltpu.CompilerParams(collective_id=0, has_side_effects=True, vmem_limit_bytes=60 << 20),
        name="radar",
    )(ref_signal, surveillance, steering, table)


def solution(mesh):
    placed = (P(None, "tm"), P(None, "chan", "tm"), P(None, None, "chan"))
    return jax.shard_map(
        on_device,
        mesh=mesh,
        in_specs=placed,
        out_specs=P("chan", None, "tm", None),
        check_vma=False,
    )
```

```python
import functools
import math

import jax
import jax.numpy as jnp
import numpy as np
from jax import lax
from jax.experimental import pallas as pl
from jax.experimental.pallas import tpu as pltpu
from jax.sharding import PartitionSpec as P

LAGS = 256
DOPPLER = 256
TAPS = 64
BLOCK = 256
HALO = 256
MESH = pl.DeviceIdType.MESH
HIGHEST = lax.Precision.HIGHEST


def dot(a, b):
    return lax.dot_general(a, b, (((1,), (0,)), ((), ())), precision=HIGHEST, preferred_element_type=jnp.float32)


def dot_nt(a, b):
    return lax.dot_general(a, b, (((1,), (1,)), ((), ())), precision=HIGHEST, preferred_element_type=jnp.float32)


def bdot(a, b):
    return lax.dot_general(a, b, (((1,), (0,)), ((), ())), preferred_element_type=jnp.float32)


def bdot_nt(a, b):
    return lax.dot_general(a, b, (((1,), (1,)), ((), ())), preferred_element_type=jnp.float32)


def split(x, terms):
    out = []
    for _ in range(terms):
        head = x.astype(jnp.bfloat16).astype(jnp.float32)
        out.append(head)
        x = x - head
    return out


def iota(shape, dim):
    return lax.broadcasted_iota(jnp.int32, shape, dim)


def conj_pack(a, b):
    half = a.shape[1] // 2
    sign = jnp.where(iota(a.shape, 1) < half, 1.0, -1.0)
    return sign * a + pltpu.roll(b, half, 1)


def widen(packed):
    half = packed.shape[1] // 2
    sign = jnp.where(iota(packed.shape, 1) < half, 1.0, -1.0)
    return jnp.concatenate([packed * sign, pltpu.roll(packed, half, 1)], 0)


def hermitian_inverse(m):
    n = m.shape[0]
    wide = (n, 2 * n)
    lane = iota((1, 2 * n), 1)
    row_id = iota((n, 1), 0)
    flip = jnp.where(lane < n, -1.0, 1.0)
    for k in range(0, n, 2):
        c0r, c1r, c0i, c1i = (jnp.broadcast_to(m[:, j : j + 1], wide) for j in (k, k + 1, n + k, n + k + 1))
        a, d = c0r[k : k + 1], c1r[k + 1 : k + 2]
        br, bi = c1r[k : k + 1], c1i[k : k + 1]
        inv = 1.0 / (a * d - (br * br + bi * bi))
        at0, at1 = lane == k, lane == k + 1
        here = at0 | at1 | (lane == n + k) | (lane == n + k + 1)
        r0 = jnp.where(here, jnp.where(at0, 1.0, 0.0), m[k : k + 1])
        r1 = jnp.where(here, jnp.where(at1, 1.0, 0.0), m[k + 1 : k + 2])
        t0 = pltpu.roll(r0, n, 1) * flip
        t1 = pltpu.roll(r1, n, 1) * flip
        n0 = d * r0 - br * r1 - bi * t1
        u0 = d * t0 - br * t1 + bi * r1
        n1 = a * r1 - br * r0 + bi * t0
        u1 = a * t1 - br * t0 - bi * r0
        change = (c0r * n0 + c1r * n1) + (c0i * u0 + c1i * u1)
        rest = jnp.where(here, 0.0, m) - inv * change
        n0, n1 = inv * n0, inv * n1
        m = jnp.where(row_id == k, n0, jnp.where(row_id == k + 1, n1, rest))
    return m


def gram_matrix(g_row, e_row):
    n = TAPS
    row = iota((n, 2 * n), 0)
    lane = iota((n, 2 * n), 1)
    col = lane % n
    sign = jnp.where(lane < n, 1.0, -1.0)

    def shifted(v):
        return pltpu.roll(jnp.broadcast_to(v, (n, 2 * n)), 0, 1, stride=1, stride_axis=0)

    upper = jnp.where(col >= row, shifted(g_row), 0.0)
    flipped = jnp.concatenate([upper, jnp.zeros_like(upper)], 0).T
    lower = flipped[:n] - pltpu.roll(flipped[n:], n, 1)
    toeplitz = jnp.where(col >= row, upper, lower)
    tail = jnp.where((col >= row) & (row >= 1), shifted(e_row), 0.0)
    tail = jnp.concatenate([tail, jnp.zeros_like(tail)], 0)
    square = dot(tail.T, tail)
    return toeplitz - (square[:n] + sign * pltpu.roll(square[n:], n, 1))


def kernel(nc, nt, ref_hbm, surv_hbm, w_hbm, table_hbm, out_ref,
           ref_ref, surv_ref, w_ref, table, part, core_buf, chip_send, chip_buf, halo, lag_hi, lag_mid, tap_lo, gm, gm_buf, xm, xm_buf, emb, lg, lg_buf,
           reach, halo_ss, halo_rs, core_ss, core_rs, rs_ss, rs_rs, gm_ss, gm_rs, xm_ss, xm_rs, lg_ss, lg_rs, in_sems):
    c = lax.axis_index("chan")
    d = lax.axis_index("tm")
    length = ref_ref.shape[1]
    beams = part.shape[2] // 2
    chips = nc // 2
    core, chip = c % 2, c // 2
    partner = c + 1 - 2 * core
    blocks = length // BLOCK

    def tm_peer(j):
        return lax.rem(d + nt // 2 + (1 - 2 * (j % 2)) * ((j + 1) // 2) + nt, nt)

    def chan_peer(j):
        return lax.rem(c + 1 + j, nc)

    barrier = pltpu.get_barrier_semaphore()

    def greet_chan(j, _):
        pl.semaphore_signal(barrier, inc=1, device_id={"chan": chan_peer(j)}, device_id_type=MESH)
        return 0

    def tm_near(offset):
        return {"tm": lax.rem(d + offset + nt, nt)}

    lax.fori_loop(0, nc - 1, greet_chan, 0)
    for offset in (-2, -1, 1, 2):
        pl.semaphore_signal(barrier, inc=1, device_id=tm_near(offset), device_id_type=MESH)

    def reach_signal(i):
        for offset in (-(2 << i), 2 << i):
            pl.semaphore_signal(reach.at[i], inc=1, device_id=tm_near(offset), device_id_type=MESH)

    def reach_wait(i):
        pl.semaphore_wait(reach.at[i], 2)

    loads = [
        pltpu.make_async_copy(source, target, in_sems.at[i])
        for i, (source, target) in enumerate(
            ((w_hbm, w_ref), (surv_hbm, surv_ref), (ref_hbm, ref_ref), (table_hbm, table)))
    ]
    for load in loads:
        load.start()
    table_copy = loads.pop()
    for load in loads:
        load.wait()

    w_re, w_im = w_ref[0], w_ref[1]
    weights_t = jnp.concatenate(
        [jnp.concatenate([w_re, w_im], 1), jnp.concatenate([-w_im, w_re], 1)], 0)
    w_hi, w_mid, w_lo = split(weights_t, 3)
    survey = jnp.concatenate([surv_ref[0], surv_ref[1]], 0)
    s_hi, s_mid, s_lo = split(survey, 3)
    left = jnp.concatenate([w_hi, w_hi, w_mid, w_hi, w_mid, w_lo], 0)
    depth = left.shape[0]
    left = jnp.concatenate([left, jnp.zeros((256 - depth, left.shape[1]), jnp.float32)], 0).T
    right_side = jnp.concatenate(
        [s_hi, s_mid, s_hi, s_lo, s_mid, s_hi, jnp.zeros((256 - depth, length), jnp.float32)], 0)
    partial = bdot(left.astype(jnp.bfloat16), right_side.astype(jnp.bfloat16))
    part_re, part_im = partial[: beams * nc], partial[beams * nc :]
    for owner in range(nc):
        rows = slice(beams * owner, beams * (owner + 1))
        part[owner % 2, owner // 2] = jnp.concatenate([part_re[rows], part_im[rows]], 0)

    pl.semaphore_wait(barrier, nc - 1 + 4)
    reach_signal(0)

    right = lax.rem(d + 1, nt)
    halo_copy = pltpu.make_async_remote_copy(
        src_ref=ref_ref.at[:, pl.ds(length - HALO, HALO)], dst_ref=halo, send_sem=halo_ss, recv_sem=halo_rs,
        device_id={"tm": right}, device_id_type=MESH)
    halo_copy.start()

    def chip_peer(j):
        return lax.rem(chip + 1 + j, chips)

    def core_copy(j):
        return pltpu.make_async_remote_copy(
            src_ref=part.at[1 - core, j], dst_ref=core_buf.at[j], send_sem=core_ss.at[j], recv_sem=core_rs.at[j],
            device_id={"chan": partner}, device_id_type=MESH)

    def rs_copy(peer, slot):
        return pltpu.make_async_remote_copy(
            src_ref=chip_send.at[peer], dst_ref=chip_buf.at[slot], send_sem=rs_ss.at[peer], recv_sem=rs_rs.at[slot],
            device_id={"chan": 2 * peer + core}, device_id_type=MESH)

    def core_start(j, _):
        core_copy(chip_peer(j)).start()
        return 0

    lax.fori_loop(0, chips, core_start, 0)

    def rs_start(j, _):
        peer = chip_peer(j)
        core_copy(peer).wait_recv()
        chip_send[peer] = part[core, peer] + core_buf[peer]
        rs_copy(peer, chip).start()
        return 0

    reach_wait(0)
    reach_signal(1)

    halo_copy.wait()
    ref = ref_ref[...]
    before = jnp.where(d == 0, 0.0, halo[...])
    extended = jnp.concatenate([before, ref], 1)

    def lags_of(p, first, count):
        row = jnp.broadcast_to(extended[p : p + 1, :], (count, HALO + length))
        return pltpu.roll(row, first, 1, stride=1, stride_axis=0)[:, HALO:]

    taps = jnp.concatenate([lags_of(0, 0, TAPS), lags_of(1, 0, TAPS)], 0)
    taps_hi, taps_mid, taps_lo = split(taps, 3)
    for p in range(2):
        lag_hi[LAGS * p : LAGS * p + TAPS] = taps_hi[TAPS * p : TAPS * (p + 1)].astype(jnp.bfloat16)
        lag_mid[LAGS * p : LAGS * p + TAPS] = taps_mid[TAPS * p : TAPS * (p + 1)].astype(jnp.bfloat16)
    tap_lo[...] = taps_lo.astype(jnp.bfloat16)

    lax.fori_loop(0, chips - 1, rs_start, 0)
    reach_wait(1)
    reach_signal(2)
    core_copy(chip).wait_recv()
    chip_buf[chip] = part[core, chip] + core_buf[chip]

    tap_terms = [jnp.concatenate([lag_hi[:TAPS], lag_hi[LAGS : LAGS + TAPS]], 0),
                 jnp.concatenate([lag_mid[:TAPS], lag_mid[LAGS : LAGS + TAPS]], 0), tap_lo[...]]

    def lag_products(rows8):
        terms = jnp.concatenate(split(rows8, 3), 0).astype(jnp.bfloat16)
        cols = sum(bdot_nt(term, terms) for term in tap_terms)
        turned = jnp.concatenate([cols, jnp.zeros((2 * TAPS, 128 - cols.shape[1]), jnp.float32)], 1).T
        return turned[:8] + turned[8:16] + turned[16:24]

    row8 = iota((8, length), 0)
    mark = jnp.where((iota((8, length), 1) == length - 1) & (d == nt - 1), 1.0, 0.0)
    probe = jnp.where(row8 == 0, ref[0:1], jnp.where(row8 == 1, ref[1:2], jnp.where(row8 == 2, mark, 0.0)))
    g_raw = lag_products(probe)
    g_conj = conj_pack(g_raw[0:1], g_raw[1:2])
    gm[0:1, :] = jnp.where(iota(g_conj.shape, 1) < TAPS, g_conj, -g_conj)
    gm[1:2, :] = g_raw[2:3]

    def gm_copy(peer, slot):
        return pltpu.make_async_remote_copy(
            src_ref=gm, dst_ref=gm_buf.at[slot], send_sem=gm_ss, recv_sem=gm_rs,
            device_id={"tm": peer}, device_id_type=MESH)

    def xm_copy(peer, slot):
        return pltpu.make_async_remote_copy(
            src_ref=xm, dst_ref=xm_buf.at[slot], send_sem=xm_ss, recv_sem=xm_rs,
            device_id={"tm": peer}, device_id_type=MESH)

    def lg_copy(peer, slot):
        return pltpu.make_async_remote_copy(
            src_ref=lg.at[peer], dst_ref=lg_buf.at[slot], send_sem=lg_ss, recv_sem=lg_rs,
            device_id={"tm": peer}, device_id_type=MESH)

    def tm_start(copy):
        for j in range(nt - 1):
            copy(tm_peer(j), d).start()

    def all_of(buf, send_sem, recv_sem):
        return pltpu.make_async_remote_copy(
            src_ref=buf.at[pl.ds(0, nt - 1)], dst_ref=buf.at[pl.ds(0, nt - 1)], send_sem=send_sem, recv_sem=recv_sem,
            device_id={"tm": tm_peer(0)}, device_id_type=MESH)

    gm_all = all_of(gm_buf, gm_ss, gm_rs)
    xm_all = all_of(xm_buf, xm_ss, xm_rs)
    lg_all = all_of(lg_buf, lg_ss, lg_rs)

    reach_wait(2)
    tm_start(gm_copy)
    gm_buf[d] = gm[...]

    for p in range(2):
        hi, mid = split(lags_of(p, TAPS, LAGS - TAPS), 2)
        lag_hi[LAGS * p + TAPS : LAGS * (p + 1)] = hi.astype(jnp.bfloat16)
        lag_mid[LAGS * p + TAPS : LAGS * (p + 1)] = mid.astype(jnp.bfloat16)

    def rs_wait(j, _):
        peer = chip_peer(j)
        rs_copy(peer, peer).wait_recv()
        return 0

    lax.fori_loop(0, chips - 1, rs_wait, 0)
    total = chip_buf[0]
    for source in range(1, chips):
        total = total + chip_buf[source]

    x_raw = lag_products(total)
    xm[...] = conj_pack(x_raw[:beams], x_raw[beams:])
    tm_start(xm_copy)
    xm_buf[d] = xm[...]

    gm_all.wait_recv()
    g_sum = jnp.sum(gm_buf[...], axis=0)
    gram = gram_matrix(g_sum[0:1], g_sum[1:2])
    level = 1.0 / gram[0:1, 0:1]
    gram = gram * level
    inverse = widen(hermitian_inverse(gram))
    gram_wide = widen(gram)

    xm_all.wait_recv()
    x = jnp.sum(xm_buf[...], axis=0) * level
    weights = dot(x, inverse)
    weights = weights + dot(x - dot(weights, gram_wide), inverse)

    sign = jnp.where(iota(weights.shape, 1) < TAPS, 1.0, -1.0)
    both = jnp.concatenate([weights * sign, pltpu.roll(weights, TAPS, 1)], 0)
    both_terms = jnp.concatenate(split(both, 3), 0).astype(jnp.bfloat16)
    model = sum(bdot(both_terms, term) for term in tap_terms)
    clean = total - (model[: 2 * beams] + model[2 * beams : 4 * beams] + model[4 * beams : 6 * beams])

    inside = iota((blocks, length), 1) // BLOCK == iota((blocks, length), 0)
    cols = 2 * blocks * beams

    def spread(row):
        return jnp.where(inside, jnp.broadcast_to(row, (blocks, length)), 0.0)

    for order, term in enumerate(split(clean, 2)):
        for m in range(beams):
            base = cols * order + 2 * blocks * m
            pair = jnp.concatenate([spread(term[m : m + 1]), spread(term[beams + m : beams + m + 1])], 0)
            emb[base : base + 2 * blocks, :] = pair.astype(jnp.bfloat16)
    own = LAGS // nt
    half = own // 2
    groups = 4
    span = LAGS // groups
    targets = nt // groups
    real_lane = iota((span, 2 * cols), 1) % (2 * blocks) < blocks
    low_lane = iota((half, 2 * cols), 1) < cols

    def correlate(step, _):
        group = lax.rem(d // targets + groups // 2 + step, groups)

        def both_terms_of(p):
            rows = pl.ds(pl.multiple_of(LAGS * p + span * group, span), span)
            sums = bdot_nt(lag_hi[rows, :], emb[...]) + bdot_nt(lag_mid[rows, :], emb[...])
            return sums + pltpu.roll(sums, cols, 1)

        with_re, with_im = both_terms_of(0), both_terms_of(1)
        lagged = with_re + jnp.where(
            real_lane, pltpu.roll(with_im, 2 * cols - blocks, 1), -pltpu.roll(with_im, blocks, 1))
        for i in range(targets):
            lg[targets * group + i] = jnp.where(
                low_lane, lagged[own * i : own * i + half], lagged[own * i + half : own * (i + 1)])

        def send(i, _):
            peer = targets * group + i

            @pl.when(peer != d)
            def _():
                lg_copy(peer, d).start()

            return 0

        lax.fori_loop(0, targets, send, 0)
        return 0

    lax.fori_loop(0, groups, correlate, 0)
    lg_buf[d] = lg[d]
    lg_all.wait_recv()

    wide = 2 * blocks
    group = 128 // wide
    slot_of = iota((own, 128), 1) // wide
    upper_row = iota((own, 128), 0) < half

    def received(s):
        twice = jnp.concatenate([lg_buf[s], lg_buf[s]], 0)
        return jnp.where(upper_row, twice, pltpu.roll(twice, 64, 1))

    arrived = [received(s) for s in range(nt)]
    rows = []
    for m in range(beams):
        pieces = []
        for start in range(0, nt, group):
            acc = jnp.zeros((own, 128), jnp.float32)
            for s in range(group):
                moved = pltpu.roll(arrived[start + s], (wide * (s - m)) % 128, 1)
                acc = jnp.where(slot_of == s, moved, acc)
            pieces.append(acc)
        rows.append(jnp.concatenate(pieces, 1))
    stacked = jnp.concatenate(rows, 0)
    height = own * beams
    stacked_terms = jnp.concatenate(split(stacked, 2), 0).astype(jnp.bfloat16)
    table_copy.wait()
    spectrum = bdot(stacked_terms, table[0]) + bdot(stacked_terms, table[1])
    spectrum = spectrum[:height] + spectrum[height:]
    for m in range(beams):
        for part_id in range(2):
            out_ref[m, part_id] = spectrum[own * m : own * (m + 1), DOPPLER * part_id : DOPPLER * (part_id + 1)]

    gm_all.wait_send()
    xm_all.wait_send()
    lg_all.wait_send()

    def rs_drain(j, _):
        peer = chip_peer(j)
        rs_copy(peer, peer).wait_send()
        return 0

    def core_drain(j, _):
        core_copy(j).wait_send()
        return 0

    lax.fori_loop(0, chips - 1, rs_drain, 0)
    lax.fori_loop(0, chips, core_drain, 0)


def doppler_table(blocks_total, blocks):
    q = np.arange(blocks_total)
    angle = 2.0 * np.pi * ((q[:, None] * np.arange(DOPPLER)[None, :]) % DOPPLER) / DOPPLER
    cosine, sine = np.cos(angle), np.sin(angle)
    first = np.concatenate([cosine, -sine], 1).reshape(-1, 1, blocks, 2 * DOPPLER)
    second = np.concatenate([sine, cosine], 1).reshape(-1, 1, blocks, 2 * DOPPLER)
    scale = 0.125 / math.sqrt(blocks_total * BLOCK)
    table = np.concatenate([first, second], 1).reshape(2 * blocks_total, 2 * DOPPLER) * scale
    head = table.astype(np.float32).astype(jnp.bfloat16)
    tail = (table - head.astype(np.float64)).astype(np.float32).astype(jnp.bfloat16)
    return np.stack([head, tail])


def on_device(ref_signal, surveillance, steering):
    nc, nt = lax.axis_size("chan"), lax.axis_size("tm")
    length = ref_signal.shape[1]
    chans = surveillance.shape[1]
    beams = steering.shape[1] // nc
    blocks = length // BLOCK
    own = LAGS // nt
    table = jnp.asarray(doppler_table(nt * blocks, blocks))
    vmem = pl.BlockSpec(memory_space=pltpu.VMEM)
    f32, bf16 = jnp.float32, jnp.bfloat16
    chips = nc // 2
    return pl.pallas_call(
        functools.partial(kernel, nc, nt),
        out_shape=jax.ShapeDtypeStruct((beams, 2, own, DOPPLER), f32),
        in_specs=[pl.BlockSpec(memory_space=pltpu.HBM)] * 4,
        out_specs=vmem,
        scratch_shapes=[
            pltpu.VMEM((2, length), f32),
            pltpu.VMEM((2, chans, length), f32),
            pltpu.VMEM((2, chans, beams * nc), f32),
            pltpu.VMEM((2, 2 * nt * blocks, 2 * DOPPLER), bf16),
            pltpu.VMEM((2, chips, 2 * beams, length), f32),
            pltpu.VMEM((chips, 2 * beams, length), f32),
            pltpu.VMEM((chips, 2 * beams, length), f32),
            pltpu.VMEM((chips, 2 * beams, length), f32),
            pltpu.VMEM((2, HALO), f32),
            pltpu.VMEM((2 * LAGS, length), bf16),
            pltpu.VMEM((2 * LAGS, length), bf16),
            pltpu.VMEM((2 * TAPS, length), bf16),
            pltpu.VMEM((2, 2 * TAPS), f32),
            pltpu.VMEM((nt, 2, 2 * TAPS), f32),
            pltpu.VMEM((beams, 2 * TAPS), f32),
            pltpu.VMEM((nt, beams, 2 * TAPS), f32),
            pltpu.VMEM((4 * blocks * beams, length), bf16),
            pltpu.VMEM((nt, own // 2, 128), f32),
            pltpu.VMEM((nt, own // 2, 128), f32),
            pltpu.SemaphoreType.REGULAR((3,)),
            pltpu.SemaphoreType.DMA,
            pltpu.SemaphoreType.DMA,
            pltpu.SemaphoreType.DMA((chips,)),
            pltpu.SemaphoreType.DMA((chips,)),
            pltpu.SemaphoreType.DMA((chips,)),
            pltpu.SemaphoreType.DMA((chips,)),
            pltpu.SemaphoreType.DMA,
            pltpu.SemaphoreType.DMA,
            pltpu.SemaphoreType.DMA,
            pltpu.SemaphoreType.DMA,
            pltpu.SemaphoreType.DMA,
            pltpu.SemaphoreType.DMA,
            pltpu.SemaphoreType.DMA((4,)),
        ],
        compiler_params=pltpu.CompilerParams(collective_id=0, has_side_effects=True, vmem_limit_bytes=60 << 20),
        name="radar",
    )(ref_signal, surveillance, jnp.swapaxes(steering, 1, 2), table)


def solution(mesh):
    placed = (P(None, "tm"), P(None, "chan", "tm"), P(None, None, "chan"))
    return jax.shard_map(
        on_device,
        mesh=mesh,
        in_specs=placed,
        out_specs=P("chan", None, "tm", None),
        check_vma=False,
    )
```

```python
import functools
import math

import jax
import jax.numpy as jnp
import numpy as np
from jax import lax
from jax.experimental import pallas as pl
from jax.experimental.pallas import tpu as pltpu
from jax.sharding import PartitionSpec as P

LAGS = 256
DOPPLER = 256
TAPS = 64
BLOCK = 256
HALO = 256
MESH = pl.DeviceIdType.MESH
HIGHEST = lax.Precision.HIGHEST


def dot(a, b):
    return lax.dot_general(a, b, (((1,), (0,)), ((), ())), precision=HIGHEST, preferred_element_type=jnp.float32)


def dot_nt(a, b):
    return lax.dot_general(a, b, (((1,), (1,)), ((), ())), precision=HIGHEST, preferred_element_type=jnp.float32)


def bdot(a, b):
    return lax.dot_general(a, b, (((1,), (0,)), ((), ())), preferred_element_type=jnp.float32)


def bdot_nt(a, b):
    return lax.dot_general(a, b, (((1,), (1,)), ((), ())), preferred_element_type=jnp.float32)


def split(x, terms):
    out = []
    for _ in range(terms):
        head = x.astype(jnp.bfloat16).astype(jnp.float32)
        out.append(head)
        x = x - head
    return out


def iota(shape, dim):
    return lax.broadcasted_iota(jnp.int32, shape, dim)


def conj_pack(a, b):
    half = a.shape[1] // 2
    sign = jnp.where(iota(a.shape, 1) < half, 1.0, -1.0)
    return sign * a + pltpu.roll(b, half, 1)


def widen(packed):
    half = packed.shape[1] // 2
    sign = jnp.where(iota(packed.shape, 1) < half, 1.0, -1.0)
    return jnp.concatenate([packed * sign, pltpu.roll(packed, half, 1)], 0)


def conj_product(left, right):
    n = left.shape[1] // 2
    pad = jnp.zeros((2 * n - left.shape[0], 2 * n), jnp.float32)
    square = dot(jnp.concatenate([left, pad], 0).T, jnp.concatenate([right, pad], 0))
    sign = jnp.where(iota((n, 2 * n), 1) < n, 1.0, -1.0)
    return square[:n] + sign * pltpu.roll(square[n:], n, 1)


def hermitian_inverse(m, scaled):
    n = m.shape[0]
    tile = 8
    blocks = [m[tile * i : tile * (i + 1)] for i in range(n // tile)]
    lane = iota((1, 2 * n), 1)
    row_id = iota((tile, 1), 0)
    flip = jnp.where(lane < n, -1.0, 1.0)
    for k in range(0, n, 2):
        home, at = blocks[k // tile], k % tile
        p0, p1 = home[at : at + 1], home[at + 1 : at + 2]
        a, br, bi = (jnp.broadcast_to(p0[:, j : j + 1], (1, 2 * n)) for j in (k, k + 1, n + k + 1))
        d = jnp.broadcast_to(p1[:, k + 1 : k + 2], (1, 2 * n))
        inv = 1.0 / (a * d - (br * br + bi * bi))
        at0, at1 = lane == k, lane == k + 1
        here = at0 | at1 | (lane == n + k) | (lane == n + k + 1)
        r0 = jnp.where(here, jnp.where(at0, 1.0, 0.0), p0)
        r1 = jnp.where(here, jnp.where(at1, 1.0, 0.0), p1)
        t0 = pltpu.roll(r0, n, 1) * flip
        t1 = pltpu.roll(r1, n, 1) * flip
        n0 = d * r0 - br * r1 - bi * t1
        u0 = d * t0 - br * t1 + bi * r1
        n1 = a * r1 - br * r0 + bi * t0
        u1 = a * t1 - br * t0 - bi * r0
        scaled[k : k + 1] = inv * n0
        scaled[k + 1 : k + 2] = inv * n1
        for i in range((k + 2) // tile, n // tile):
            block = blocks[i]
            c0r, c1r, c0i, c1i = (
                jnp.broadcast_to(block[:, j : j + 1], (tile, 2 * n)) for j in (k, k + 1, n + k, n + k + 1))
            change = (c0r * n0 + c1r * n1) + (c0i * u0 + c1i * u1)
            rest = jnp.where(here, 0.0, block) - inv * change
            blocks[i] = rest if tile * i > k + 1 else jnp.where(row_id > at + 1, rest, block)
    row = iota((n, 2 * n), 0)
    col = iota((n, 2 * n), 1) % n
    whole = jnp.concatenate(blocks, 0)
    lower = jnp.where(col < row - row % 2, whole, jnp.where(iota((n, 2 * n), 1) == row, 1.0, 0.0))
    return conj_product(lower, jnp.where(col < row - row % 2 + 2, scaled[...], 0.0))


def gram_matrix(g_row, e_row):
    n = TAPS
    row = iota((n, 2 * n), 0)
    lane = iota((n, 2 * n), 1)
    col = lane % n

    def shifted(v):
        return pltpu.roll(jnp.broadcast_to(v, (n, 2 * n)), 0, 1, stride=1, stride_axis=0)

    upper = jnp.where(col >= row, shifted(g_row), 0.0)
    flipped = jnp.concatenate([upper, jnp.zeros_like(upper)], 0).T
    lower = flipped[:n] - pltpu.roll(flipped[n:], n, 1)
    toeplitz = jnp.where(col >= row, upper, lower)
    tail = jnp.where((col >= row) & (row >= 1), shifted(e_row), 0.0)
    return toeplitz - conj_product(tail, tail)


def kernel(nc, nt, ref_hbm, surv_hbm, w_hbm, table_hbm, out_ref,
           ref_ref, surv_ref, w_ref, table, part, core_buf, chip_send, chip_buf, halo, lag_tab, gm, gm_buf, xm, xm_buf, scaled, emb, lg, lg_buf,
           reach, halo_ss, halo_rs, core_ss, core_rs, rs_ss, rs_rs, gm_ss, gm_rs, xm_ss, xm_rs, lg_ss, lg_rs, in_sems):
    c = lax.axis_index("chan")
    d = lax.axis_index("tm")
    length = ref_ref.shape[1]
    beams = part.shape[2] // 2
    chips = nc // 2
    core, chip = c % 2, c // 2
    partner = c + 1 - 2 * core
    blocks = length // BLOCK

    def tm_peer(j):
        return lax.rem(d + nt // 2 + (1 - 2 * (j % 2)) * ((j + 1) // 2) + nt, nt)

    def chan_peer(j):
        return lax.rem(c + 1 + j, nc)

    barrier = pltpu.get_barrier_semaphore()

    def greet_chan(j, _):
        pl.semaphore_signal(barrier, inc=1, device_id={"chan": chan_peer(j)}, device_id_type=MESH)
        return 0

    def tm_near(offset):
        return {"tm": lax.rem(d + offset + nt, nt)}

    for j in range(nc - 1):
        greet_chan(j, 0)
    for offset in (-2, -1, 1, 2):
        pl.semaphore_signal(barrier, inc=1, device_id=tm_near(offset), device_id_type=MESH)

    def reach_signal(i):
        for offset in (-(2 << i), 2 << i):
            pl.semaphore_signal(reach.at[i], inc=1, device_id=tm_near(offset), device_id_type=MESH)

    def reach_wait(i):
        pl.semaphore_wait(reach.at[i], 2)

    loads = [
        pltpu.make_async_copy(source, target, in_sems.at[i])
        for i, (source, target) in enumerate(
            ((w_hbm, w_ref), (surv_hbm, surv_ref), (ref_hbm, ref_ref), (table_hbm, table)))
    ]
    for load in loads:
        load.start()
    table_copy = loads.pop()
    for load in loads:
        load.wait()

    w_re, w_im = w_ref[0], w_ref[1]
    weights_t = jnp.concatenate(
        [jnp.concatenate([w_re, w_im], 1), jnp.concatenate([-w_im, w_re], 1)], 0)
    w_hi, w_mid, w_lo = split(weights_t, 3)
    survey = jnp.concatenate([surv_ref[0], surv_ref[1]], 0)
    s_hi, s_mid, s_lo = split(survey, 3)
    left = jnp.concatenate([w_hi, w_hi, w_mid, w_hi, w_mid, w_lo], 0)
    depth = left.shape[0]
    left = jnp.concatenate([left, jnp.zeros((256 - depth, left.shape[1]), jnp.float32)], 0).T
    right_side = jnp.concatenate(
        [s_hi, s_mid, s_hi, s_lo, s_mid, s_hi, jnp.zeros((256 - depth, length), jnp.float32)], 0)
    partial = bdot(left.astype(jnp.bfloat16), right_side.astype(jnp.bfloat16))
    part_re, part_im = partial[: beams * nc], partial[beams * nc :]
    for owner in range(nc):
        rows = slice(beams * owner, beams * (owner + 1))
        part[owner % 2, owner // 2] = jnp.concatenate([part_re[rows], part_im[rows]], 0)

    pl.semaphore_wait(barrier, nc - 1 + 4)
    reach_signal(0)

    right = lax.rem(d + 1, nt)
    halo_copy = pltpu.make_async_remote_copy(
        src_ref=ref_ref.at[:, pl.ds(length - HALO, HALO)], dst_ref=halo, send_sem=halo_ss, recv_sem=halo_rs,
        device_id={"tm": right}, device_id_type=MESH)
    halo_copy.start()

    def chip_peer(j):
        return lax.rem(chip + 1 + j, chips)

    def core_copy(j):
        return pltpu.make_async_remote_copy(
            src_ref=part.at[1 - core, j], dst_ref=core_buf.at[j], send_sem=core_ss.at[j], recv_sem=core_rs.at[j],
            device_id={"chan": partner}, device_id_type=MESH)

    def rs_copy(peer, slot):
        return pltpu.make_async_remote_copy(
            src_ref=chip_send.at[peer], dst_ref=chip_buf.at[slot], send_sem=rs_ss.at[peer], recv_sem=rs_rs.at[slot],
            device_id={"chan": 2 * peer + core}, device_id_type=MESH)

    def core_start(j, _):
        core_copy(chip_peer(j)).start()
        return 0

    for j in range(chips):
        core_start(j, 0)

    def rs_start(j, _):
        peer = chip_peer(j)
        core_copy(peer).wait_recv()
        chip_send[peer] = part[core, peer] + core_buf[peer]
        rs_copy(peer, chip).start()
        return 0

    reach_wait(0)
    reach_signal(1)

    halo_copy.wait()
    ref = ref_ref[...]
    before = jnp.where(d == 0, 0.0, halo[...])
    extended = jnp.concatenate([before, ref], 1)

    def lags_of(p, first, count):
        row = jnp.broadcast_to(extended[p : p + 1, :], (count, HALO + length))
        return pltpu.roll(row, first, 1, stride=1, stride_axis=0)[:, HALO:]

    taps = jnp.concatenate([lags_of(0, 0, TAPS), lags_of(1, 0, TAPS)], 0)
    taps_hi, taps_mid, taps_lo = split(taps, 3)
    for order, term in enumerate((taps_lo, taps_hi, taps_mid)):
        lag_tab[2 * TAPS * order : 2 * TAPS * (order + 1)] = term.astype(jnp.bfloat16)

    for j in range(chips - 1):
        rs_start(j, 0)
    reach_wait(1)
    reach_signal(2)
    core_copy(chip).wait_recv()
    chip_buf[chip] = part[core, chip] + core_buf[chip]

    tap_rows = 6 * TAPS

    def lag_products(rows8):
        terms = jnp.concatenate(split(rows8, 3), 0).astype(jnp.bfloat16)
        cols = bdot_nt(lag_tab[:tap_rows], terms)
        cols = cols[: 2 * TAPS] + cols[2 * TAPS : 4 * TAPS] + cols[4 * TAPS :]
        turned = jnp.concatenate([cols, jnp.zeros((2 * TAPS, 128 - cols.shape[1]), jnp.float32)], 1).T
        return turned[:8] + turned[8:16] + turned[16:24]

    row8 = iota((8, length), 0)
    mark = jnp.where((iota((8, length), 1) == length - 1) & (d == nt - 1), 1.0, 0.0)
    probe = jnp.where(row8 == 0, ref[0:1], jnp.where(row8 == 1, ref[1:2], jnp.where(row8 == 2, mark, 0.0)))
    g_raw = lag_products(probe)
    g_conj = conj_pack(g_raw[0:1], g_raw[1:2])
    gm[0:1, :] = jnp.where(iota(g_conj.shape, 1) < TAPS, g_conj, -g_conj)
    gm[1:2, :] = g_raw[2:3]

    def gm_copy(peer, slot):
        return pltpu.make_async_remote_copy(
            src_ref=gm, dst_ref=gm_buf.at[slot], send_sem=gm_ss, recv_sem=gm_rs,
            device_id={"tm": peer}, device_id_type=MESH)

    def xm_copy(peer, slot):
        return pltpu.make_async_remote_copy(
            src_ref=xm, dst_ref=xm_buf.at[slot], send_sem=xm_ss, recv_sem=xm_rs,
            device_id={"tm": peer}, device_id_type=MESH)

    def lg_copy(peer, slot):
        return pltpu.make_async_remote_copy(
            src_ref=lg.at[peer], dst_ref=lg_buf.at[slot], send_sem=lg_ss, recv_sem=lg_rs,
            device_id={"tm": peer}, device_id_type=MESH)

    def tm_start(copy):
        for j in range(nt - 1):
            copy(tm_peer(j), d).start()

    def all_of(buf, send_sem, recv_sem):
        return pltpu.make_async_remote_copy(
            src_ref=buf.at[pl.ds(0, nt - 1)], dst_ref=buf.at[pl.ds(0, nt - 1)], send_sem=send_sem, recv_sem=recv_sem,
            device_id={"tm": tm_peer(0)}, device_id_type=MESH)

    gm_all = all_of(gm_buf, gm_ss, gm_rs)
    xm_all = all_of(xm_buf, xm_ss, xm_rs)
    lg_all = all_of(lg_buf, lg_ss, lg_rs)

    reach_wait(2)
    tm_start(gm_copy)
    gm_buf[d] = gm[...]

    for p in range(2):
        hi, mid = split(lags_of(p, TAPS, LAGS - TAPS), 2)
        for group in range(1, LAGS // TAPS):
            rows = slice(TAPS * (group - 1), TAPS * group)
            base = 2 * TAPS + 4 * TAPS * group + TAPS * p
            lag_tab[base : base + TAPS] = hi[rows].astype(jnp.bfloat16)
            lag_tab[base + 2 * TAPS : base + 3 * TAPS] = mid[rows].astype(jnp.bfloat16)

    def rs_wait(j, _):
        peer = chip_peer(j)
        rs_copy(peer, peer).wait_recv()
        return 0

    for j in range(chips - 1):
        rs_wait(j, 0)
    total = chip_buf[0]
    for source in range(1, chips):
        total = total + chip_buf[source]

    x_raw = lag_products(total)
    xm[...] = conj_pack(x_raw[:beams], x_raw[beams:])
    tm_start(xm_copy)
    xm_buf[d] = xm[...]

    gm_all.wait_recv()
    g_sum = jnp.sum(gm_buf[...], axis=0)
    gram = gram_matrix(g_sum[0:1], g_sum[1:2])
    level = 1.0 / gram[0:1, 0:1]
    gram = gram * level
    inverse = widen(hermitian_inverse(gram, scaled))
    gram_wide = widen(gram)

    xm_all.wait_recv()
    x = jnp.sum(xm_buf[...], axis=0) * level
    weights = dot(x, inverse)
    weights = weights + dot(x - dot(weights, gram_wide), inverse)

    sign = jnp.where(iota(weights.shape, 1) < TAPS, 1.0, -1.0)
    both = jnp.concatenate([weights * sign, pltpu.roll(weights, TAPS, 1)], 0)
    both_terms = jnp.concatenate(split(both, 3), 0).astype(jnp.bfloat16)
    model = bdot(jnp.concatenate([both_terms] * 3, 1), lag_tab[:tap_rows])
    clean = total - (model[: 2 * beams] + model[2 * beams : 4 * beams] + model[4 * beams : 6 * beams])

    inside = iota((blocks, length), 1) // BLOCK == iota((blocks, length), 0)
    cols = 2 * blocks * beams

    def spread(row):
        return jnp.where(inside, jnp.broadcast_to(row, (blocks, length)), 0.0)

    for order, term in enumerate(split(clean, 2)):
        for m in range(beams):
            base = cols * order + 2 * blocks * m
            pair = jnp.concatenate([spread(term[m : m + 1]), spread(term[beams + m : beams + m + 1])], 0)
            emb[base : base + 2 * blocks, :] = pair.astype(jnp.bfloat16)
    own = LAGS // nt
    half = own // 2
    groups = 4
    span = LAGS // groups
    targets = nt // groups
    real_lane = iota((span, 2 * cols), 1) % (2 * blocks) < blocks
    low_lane = iota((half, 2 * cols), 1) < cols

    def correlate(step, _):
        group = lax.rem(d // targets + groups // 2 + step, groups)

        sums = bdot_nt(lag_tab[pl.ds(pl.multiple_of(2 * TAPS + 4 * span * group, 2 * TAPS), 4 * span), :], emb[...])
        sums = sums[: 2 * span] + sums[2 * span :]
        sums = sums + pltpu.roll(sums, cols, 1)
        with_re, with_im = sums[:span], sums[span:]
        lagged = with_re + jnp.where(
            real_lane, pltpu.roll(with_im, 2 * cols - blocks, 1), -pltpu.roll(with_im, blocks, 1))
        for i in range(targets):
            lg[targets * group + i] = jnp.where(
                low_lane, lagged[own * i : own * i + half], lagged[own * i + half : own * (i + 1)])

        for i in range(targets):
            peer = targets * group + i

            @pl.when(peer != d)
            def _(peer=peer):
                lg_copy(peer, d).start()

        return 0

    lax.fori_loop(0, groups, correlate, 0)
    lg_buf[d] = lg[d]
    gm_all.wait_send()
    xm_all.wait_send()

    def rs_drain(j, _):
        peer = chip_peer(j)
        rs_copy(peer, peer).wait_send()
        return 0

    def core_drain(j, _):
        core_copy(j).wait_send()
        return 0

    lax.fori_loop(0, chips - 1, rs_drain, 0)
    lax.fori_loop(0, chips, core_drain, 0)
    lg_all.wait_recv()

    wide = 2 * blocks
    group = 128 // wide
    slot_of = iota((own, 128), 1) // wide
    upper_row = iota((own, 128), 0) < half

    def received(s):
        twice = jnp.concatenate([lg_buf[s], lg_buf[s]], 0)
        return jnp.where(upper_row, twice, pltpu.roll(twice, 64, 1))

    arrived = [received(s) for s in range(nt)]
    rows = []
    for m in range(beams):
        pieces = []
        for start in range(0, nt, group):
            acc = jnp.zeros((own, 128), jnp.float32)
            for s in range(group):
                moved = pltpu.roll(arrived[start + s], (wide * (s - m)) % 128, 1)
                acc = jnp.where(slot_of == s, moved, acc)
            pieces.append(acc)
        rows.append(jnp.concatenate(pieces, 1))
    stacked = jnp.concatenate(rows, 0)
    height = own * beams
    stacked_terms = jnp.concatenate(split(stacked, 2), 0).astype(jnp.bfloat16)
    table_copy.wait()
    spectrum = bdot(stacked_terms, table[0]) + bdot(stacked_terms, table[1])
    spectrum = spectrum[:height] + spectrum[height:]
    for m in range(beams):
        for part_id in range(2):
            out_ref[m, part_id] = spectrum[own * m : own * (m + 1), DOPPLER * part_id : DOPPLER * (part_id + 1)]

    lg_all.wait_send()


def doppler_table(blocks_total, blocks):
    q = np.arange(blocks_total)
    angle = 2.0 * np.pi * ((q[:, None] * np.arange(DOPPLER)[None, :]) % DOPPLER) / DOPPLER
    cosine, sine = np.cos(angle), np.sin(angle)
    first = np.concatenate([cosine, -sine], 1).reshape(-1, 1, blocks, 2 * DOPPLER)
    second = np.concatenate([sine, cosine], 1).reshape(-1, 1, blocks, 2 * DOPPLER)
    scale = 0.125 / math.sqrt(blocks_total * BLOCK)
    table = np.concatenate([first, second], 1).reshape(2 * blocks_total, 2 * DOPPLER) * scale
    head = table.astype(np.float32).astype(jnp.bfloat16)
    tail = (table - head.astype(np.float64)).astype(np.float32).astype(jnp.bfloat16)
    return np.stack([head, tail])


def on_device(ref_signal, surveillance, steering):
    nc, nt = lax.axis_size("chan"), lax.axis_size("tm")
    length = ref_signal.shape[1]
    chans = surveillance.shape[1]
    beams = steering.shape[1] // nc
    blocks = length // BLOCK
    own = LAGS // nt
    table = jnp.asarray(doppler_table(nt * blocks, blocks))
    vmem = pl.BlockSpec(memory_space=pltpu.VMEM)
    f32, bf16 = jnp.float32, jnp.bfloat16
    chips = nc // 2
    return pl.pallas_call(
        functools.partial(kernel, nc, nt),
        out_shape=jax.ShapeDtypeStruct((beams, 2, own, DOPPLER), f32),
        in_specs=[pl.BlockSpec(memory_space=pltpu.HBM)] * 4,
        out_specs=vmem,
        scratch_shapes=[
            pltpu.VMEM((2, length), f32),
            pltpu.VMEM((2, chans, length), f32),
            pltpu.VMEM((2, chans, beams * nc), f32),
            pltpu.VMEM((2, 2 * nt * blocks, 2 * DOPPLER), bf16),
            pltpu.VMEM((2, chips, 2 * beams, length), f32),
            pltpu.VMEM((chips, 2 * beams, length), f32),
            pltpu.VMEM((chips, 2 * beams, length), f32),
            pltpu.VMEM((chips, 2 * beams, length), f32),
            pltpu.VMEM((2, HALO), f32),
            pltpu.VMEM((2 * TAPS + 4 * LAGS, length), bf16),
            pltpu.VMEM((2, 2 * TAPS), f32),
            pltpu.VMEM((nt, 2, 2 * TAPS), f32),
            pltpu.VMEM((beams, 2 * TAPS), f32),
            pltpu.VMEM((nt, beams, 2 * TAPS), f32),
            pltpu.VMEM((TAPS, 2 * TAPS), f32),
            pltpu.VMEM((4 * blocks * beams, length), bf16),
            pltpu.VMEM((nt, own // 2, 128), f32),
            pltpu.VMEM((nt, own // 2, 128), f32),
            pltpu.SemaphoreType.REGULAR((3,)),
            pltpu.SemaphoreType.DMA,
            pltpu.SemaphoreType.DMA,
            pltpu.SemaphoreType.DMA((chips,)),
            pltpu.SemaphoreType.DMA((chips,)),
            pltpu.SemaphoreType.DMA((chips,)),
            pltpu.SemaphoreType.DMA((chips,)),
            pltpu.SemaphoreType.DMA,
            pltpu.SemaphoreType.DMA,
            pltpu.SemaphoreType.DMA,
            pltpu.SemaphoreType.DMA,
            pltpu.SemaphoreType.DMA,
            pltpu.SemaphoreType.DMA,
            pltpu.SemaphoreType.DMA((4,)),
        ],
        compiler_params=pltpu.CompilerParams(collective_id=0, has_side_effects=True, vmem_limit_bytes=60 << 20),
        name="radar",
    )(ref_signal, surveillance, jnp.swapaxes(steering, 1, 2), table)


def solution(mesh):
    placed = (P(None, "tm"), P(None, "chan", "tm"), P(None, None, "chan"))
    return jax.shard_map(
        on_device,
        mesh=mesh,
        in_specs=placed,
        out_specs=P("chan", None, "tm", None),
        check_vma=False,
    )
```

```python
import functools
import math

import jax
import jax.numpy as jnp
import numpy as np
from jax import lax
from jax.experimental import pallas as pl
from jax.experimental.pallas import tpu as pltpu
from jax.sharding import PartitionSpec as P

LAGS = 256
DOPPLER = 256
TAPS = 64
BLOCK = 256
HALO = 256
MESH = pl.DeviceIdType.MESH
HIGHEST = lax.Precision.HIGHEST


def dot(a, b):
    return lax.dot_general(a, b, (((1,), (0,)), ((), ())), precision=HIGHEST, preferred_element_type=jnp.float32)


def dot_nt(a, b):
    return lax.dot_general(a, b, (((1,), (1,)), ((), ())), precision=HIGHEST, preferred_element_type=jnp.float32)


def bdot(a, b):
    return lax.dot_general(a, b, (((1,), (0,)), ((), ())), preferred_element_type=jnp.float32)


def bdot_nt(a, b):
    return lax.dot_general(a, b, (((1,), (1,)), ((), ())), preferred_element_type=jnp.float32)


def split(x, terms):
    out = []
    for _ in range(terms):
        head = x.astype(jnp.bfloat16).astype(jnp.float32)
        out.append(head)
        x = x - head
    return out


def iota(shape, dim):
    return lax.broadcasted_iota(jnp.int32, shape, dim)


def conj_pack(a, b):
    half = a.shape[1] // 2
    sign = jnp.where(iota(a.shape, 1) < half, 1.0, -1.0)
    return sign * a + pltpu.roll(b, half, 1)


def widen(packed):
    half = packed.shape[1] // 2
    sign = jnp.where(iota(packed.shape, 1) < half, 1.0, -1.0)
    return jnp.concatenate([packed * sign, pltpu.roll(packed, half, 1)], 0)


def conj_product(left, right):
    n = left.shape[1] // 2
    pad = jnp.zeros((2 * n - left.shape[0], 2 * n), jnp.float32)
    square = dot(jnp.concatenate([left, pad], 0).T, jnp.concatenate([right, pad], 0))
    sign = jnp.where(iota((n, 2 * n), 1) < n, 1.0, -1.0)
    return square[:n] + sign * pltpu.roll(square[n:], n, 1)


def hermitian_inverse(m, scaled):
    n = m.shape[0]
    tile = 8
    blocks = [m[tile * i : tile * (i + 1)] for i in range(n // tile)]
    lane = iota((1, 2 * n), 1)
    row_id = iota((tile, 1), 0)
    flip = jnp.where(lane < n, -1.0, 1.0)
    for k in range(0, n, 2):
        home, at = blocks[k // tile], k % tile
        p0, p1 = home[at : at + 1], home[at + 1 : at + 2]
        a, br, bi = (jnp.broadcast_to(p0[:, j : j + 1], (1, 2 * n)) for j in (k, k + 1, n + k + 1))
        d = jnp.broadcast_to(p1[:, k + 1 : k + 2], (1, 2 * n))
        inv = 1.0 / (a * d - (br * br + bi * bi))
        at0, at1 = lane == k, lane == k + 1
        here = at0 | at1 | (lane == n + k) | (lane == n + k + 1)
        r0 = jnp.where(here, jnp.where(at0, 1.0, 0.0), p0)
        r1 = jnp.where(here, jnp.where(at1, 1.0, 0.0), p1)
        t0 = pltpu.roll(r0, n, 1) * flip
        t1 = pltpu.roll(r1, n, 1) * flip
        n0 = d * r0 - br * r1 - bi * t1
        u0 = d * t0 - br * t1 + bi * r1
        n1 = a * r1 - br * r0 + bi * t0
        u1 = a * t1 - br * t0 - bi * r0
        scaled[k : k + 1] = inv * n0
        scaled[k + 1 : k + 2] = inv * n1
        for i in range((k + 2) // tile, n // tile):
            block = blocks[i]
            c0r, c1r, c0i, c1i = (
                jnp.broadcast_to(block[:, j : j + 1], (tile, 2 * n)) for j in (k, k + 1, n + k, n + k + 1))
            change = (c0r * n0 + c1r * n1) + (c0i * u0 + c1i * u1)
            rest = jnp.where(here, 0.0, block) - inv * change
            blocks[i] = rest if tile * i > k + 1 else jnp.where(row_id > at + 1, rest, block)
    row = iota((n, 2 * n), 0)
    col = iota((n, 2 * n), 1) % n
    whole = jnp.concatenate(blocks, 0)
    lower = jnp.where(col < row - row % 2, whole, jnp.where(iota((n, 2 * n), 1) == row, 1.0, 0.0))
    return conj_product(lower, jnp.where(col < row - row % 2 + 2, scaled[...], 0.0))


def gram_matrix(g_row, e_row):
    n = TAPS
    row = iota((n, 2 * n), 0)
    lane = iota((n, 2 * n), 1)
    col = lane % n

    def shifted(v):
        return pltpu.roll(jnp.broadcast_to(v, (n, 2 * n)), 0, 1, stride=1, stride_axis=0)

    upper = jnp.where(col >= row, shifted(g_row), 0.0)
    flipped = jnp.concatenate([upper, jnp.zeros_like(upper)], 0).T
    lower = flipped[:n] - pltpu.roll(flipped[n:], n, 1)
    toeplitz = jnp.where(col >= row, upper, lower)
    tail = jnp.where((col >= row) & (row >= 1), shifted(e_row), 0.0)
    return toeplitz - conj_product(tail, tail)


def kernel(nc, nt, ref_hbm, surv_hbm, w_hbm, table_hbm, out_ref,
           ref_ref, surv_ref, w_ref, table, part, core_buf, chip_send, chip_buf, halo, lag_tab, gm, gm_buf, xm, xm_buf, scaled, emb, lg, lg_buf,
           reach, halo_ss, halo_rs, core_ss, core_rs, rs_ss, rs_rs, gm_ss, gm_rs, xm_ss, xm_rs, lg_ss, lg_rs, in_sems):
    c = lax.axis_index("chan")
    d = lax.axis_index("tm")
    length = ref_ref.shape[1]
    beams = part.shape[2] // 2
    chips = nc // 2
    core, chip = c % 2, c // 2
    partner = c + 1 - 2 * core
    blocks = length // BLOCK

    def tm_peer(j):
        return lax.rem(d + nt // 2 + (1 - 2 * (j % 2)) * ((j + 1) // 2) + nt, nt)

    def chan_peer(j):
        return lax.rem(c + 1 + j, nc)

    barrier = pltpu.get_barrier_semaphore()

    def greet_chan(j, _):
        pl.semaphore_signal(barrier, inc=1, device_id={"chan": chan_peer(j)}, device_id_type=MESH)
        return 0

    def tm_near(offset):
        return {"tm": lax.rem(d + offset + nt, nt)}

    for j in range(nc - 1):
        greet_chan(j, 0)
    for offset in (-2, -1, 1, 2):
        pl.semaphore_signal(barrier, inc=1, device_id=tm_near(offset), device_id_type=MESH)

    def reach_signal(i):
        for offset in (-(2 << i), 2 << i):
            pl.semaphore_signal(reach.at[i], inc=1, device_id=tm_near(offset), device_id_type=MESH)

    def reach_wait(i):
        pl.semaphore_wait(reach.at[i], 2)

    loads = [
        pltpu.make_async_copy(source, target, in_sems.at[i])
        for i, (source, target) in enumerate(
            ((w_hbm, w_ref), (surv_hbm, surv_ref), (ref_hbm, ref_ref), (table_hbm, table)))
    ]
    for load in loads:
        load.start()
    table_copy = loads.pop()
    for load in loads:
        load.wait()

    w_re, w_im = w_ref[0], w_ref[1]
    weights_t = jnp.concatenate(
        [jnp.concatenate([w_re, w_im], 1), jnp.concatenate([-w_im, w_re], 1)], 0)
    w_hi, w_mid, w_lo = split(weights_t, 3)
    survey = jnp.concatenate([surv_ref[0], surv_ref[1]], 0)
    s_hi, s_mid, s_lo = split(survey, 3)
    left = jnp.concatenate([w_hi, w_hi, w_mid, w_hi, w_mid, w_lo], 0)
    depth = left.shape[0]
    left = jnp.concatenate([left, jnp.zeros((256 - depth, left.shape[1]), jnp.float32)], 0).T
    right_side = jnp.concatenate(
        [s_hi, s_mid, s_hi, s_lo, s_mid, s_hi, jnp.zeros((256 - depth, length), jnp.float32)], 0)
    partial = bdot(left.astype(jnp.bfloat16), right_side.astype(jnp.bfloat16))
    part_re, part_im = partial[: beams * nc], partial[beams * nc :]
    for owner in range(nc):
        rows = slice(beams * owner, beams * (owner + 1))
        part[owner % 2, owner // 2] = jnp.concatenate([part_re[rows], part_im[rows]], 0)

    pl.semaphore_wait(barrier, nc - 1 + 4)
    reach_signal(0)

    right = lax.rem(d + 1, nt)
    halo_copy = pltpu.make_async_remote_copy(
        src_ref=ref_ref.at[:, pl.ds(length - HALO, HALO)], dst_ref=halo, send_sem=halo_ss, recv_sem=halo_rs,
        device_id={"tm": right}, device_id_type=MESH)
    halo_copy.start()

    halves = 2
    steps = chips // halves
    far_first = sorted(
        ((a, b) for a in range(halves) for b in range(steps) if a or b),
        key=lambda ab: -(2 * ab[0] + min(ab[1], steps - ab[1])))

    def chip_peer(j):
        a, b = far_first[j]
        return lax.rem(chip // steps + a, halves) * steps + lax.rem(chip % steps + b, steps)

    def core_copy(j):
        return pltpu.make_async_remote_copy(
            src_ref=part.at[1 - core, j], dst_ref=core_buf.at[j], send_sem=core_ss.at[j], recv_sem=core_rs.at[j],
            device_id={"chan": partner}, device_id_type=MESH)

    def rs_copy(peer, slot):
        return pltpu.make_async_remote_copy(
            src_ref=chip_send.at[peer], dst_ref=chip_buf.at[slot], send_sem=rs_ss.at[peer], recv_sem=rs_rs.at[slot],
            device_id={"chan": 2 * peer + core}, device_id_type=MESH)

    def core_start(j, _):
        core_copy(chip_peer(j)).start()
        return 0

    for j in range(chips - 1):
        core_start(j, 0)
    core_copy(chip).start()

    def rs_start(j, _):
        peer = chip_peer(j)
        core_copy(peer).wait_recv()
        chip_send[peer] = part[core, peer] + core_buf[peer]
        rs_copy(peer, chip).start()
        return 0

    reach_wait(0)
    reach_signal(1)

    for j in range(chips - 1):
        rs_start(j, 0)

    halo_copy.wait()
    ref = ref_ref[...]
    before = jnp.where(d == 0, 0.0, halo[...])
    extended = jnp.concatenate([before, ref], 1)

    def lags_of(p, first, count):
        row = jnp.broadcast_to(extended[p : p + 1, :], (count, HALO + length))
        return pltpu.roll(row, first, 1, stride=1, stride_axis=0)[:, HALO:]

    taps = jnp.concatenate([lags_of(0, 0, TAPS), lags_of(1, 0, TAPS)], 0)
    taps_hi, taps_mid, taps_lo = split(taps, 3)
    for order, term in enumerate((taps_lo, taps_hi, taps_mid)):
        lag_tab[2 * TAPS * order : 2 * TAPS * (order + 1)] = term.astype(jnp.bfloat16)

    reach_wait(1)
    reach_signal(2)
    core_copy(chip).wait_recv()
    chip_buf[chip] = part[core, chip] + core_buf[chip]

    tap_rows = 6 * TAPS

    def lag_products(rows8):
        terms = jnp.concatenate(split(rows8, 3), 0).astype(jnp.bfloat16)
        cols = bdot_nt(lag_tab[:tap_rows], terms)
        cols = cols[: 2 * TAPS] + cols[2 * TAPS : 4 * TAPS] + cols[4 * TAPS :]
        turned = jnp.concatenate([cols, jnp.zeros((2 * TAPS, 128 - cols.shape[1]), jnp.float32)], 1).T
        return turned[:8] + turned[8:16] + turned[16:24]

    row8 = iota((8, length), 0)
    mark = jnp.where((iota((8, length), 1) == length - 1) & (d == nt - 1), 1.0, 0.0)
    probe = jnp.where(row8 == 0, ref[0:1], jnp.where(row8 == 1, ref[1:2], jnp.where(row8 == 2, mark, 0.0)))
    g_raw = lag_products(probe)
    g_conj = conj_pack(g_raw[0:1], g_raw[1:2])
    gm[0:1, :] = jnp.where(iota(g_conj.shape, 1) < TAPS, g_conj, -g_conj)
    gm[1:2, :] = g_raw[2:3]

    def gm_copy(peer, slot):
        return pltpu.make_async_remote_copy(
            src_ref=gm, dst_ref=gm_buf.at[slot], send_sem=gm_ss, recv_sem=gm_rs,
            device_id={"tm": peer}, device_id_type=MESH)

    def xm_copy(peer, slot):
        return pltpu.make_async_remote_copy(
            src_ref=xm, dst_ref=xm_buf.at[slot], send_sem=xm_ss, recv_sem=xm_rs,
            device_id={"tm": peer}, device_id_type=MESH)

    def lg_copy(peer, slot):
        return pltpu.make_async_remote_copy(
            src_ref=lg.at[peer], dst_ref=lg_buf.at[slot], send_sem=lg_ss, recv_sem=lg_rs,
            device_id={"tm": peer}, device_id_type=MESH)

    def tm_start(copy):
        for j in range(nt - 1):
            copy(tm_peer(j), d).start()

    def all_of(buf, send_sem, recv_sem):
        return pltpu.make_async_remote_copy(
            src_ref=buf.at[pl.ds(0, nt - 1)], dst_ref=buf.at[pl.ds(0, nt - 1)], send_sem=send_sem, recv_sem=recv_sem,
            device_id={"tm": tm_peer(0)}, device_id_type=MESH)

    gm_all = all_of(gm_buf, gm_ss, gm_rs)
    xm_all = all_of(xm_buf, xm_ss, xm_rs)
    lg_all = all_of(lg_buf, lg_ss, lg_rs)

    reach_wait(2)
    tm_start(gm_copy)
    gm_buf[d] = gm[...]

    for p in range(2):
        hi, mid = split(lags_of(p, TAPS, LAGS - TAPS), 2)
        for group in range(1, LAGS // TAPS):
            rows = slice(TAPS * (group - 1), TAPS * group)
            base = 2 * TAPS + 4 * TAPS * group + TAPS * p
            lag_tab[base : base + TAPS] = hi[rows].astype(jnp.bfloat16)
            lag_tab[base + 2 * TAPS : base + 3 * TAPS] = mid[rows].astype(jnp.bfloat16)

    def rs_wait(j, _):
        peer = chip_peer(j)
        rs_copy(peer, peer).wait_recv()
        return 0

    for j in range(chips - 1):
        rs_wait(j, 0)
    total = chip_buf[0]
    for source in range(1, chips):
        total = total + chip_buf[source]

    x_raw = lag_products(total)
    xm[...] = conj_pack(x_raw[:beams], x_raw[beams:])
    tm_start(xm_copy)
    xm_buf[d] = xm[...]

    gm_all.wait_recv()
    g_sum = jnp.sum(gm_buf[...], axis=0)
    gram = gram_matrix(g_sum[0:1], g_sum[1:2])
    level = 1.0 / gram[0:1, 0:1]
    gram = gram * level
    inverse = widen(hermitian_inverse(gram, scaled))
    gram_wide = widen(gram)

    xm_all.wait_recv()
    x = jnp.sum(xm_buf[...], axis=0) * level
    weights = dot(x, inverse)
    weights = weights + dot(x - dot(weights, gram_wide), inverse)

    sign = jnp.where(iota(weights.shape, 1) < TAPS, 1.0, -1.0)
    both = jnp.concatenate([weights * sign, pltpu.roll(weights, TAPS, 1)], 0)
    both_terms = jnp.concatenate(split(both, 3), 0).astype(jnp.bfloat16)
    model = bdot(jnp.concatenate([both_terms] * 3, 1), lag_tab[:tap_rows])
    clean = total - (model[: 2 * beams] + model[2 * beams : 4 * beams] + model[4 * beams : 6 * beams])

    inside = iota((blocks, length), 1) // BLOCK == iota((blocks, length), 0)
    cols = 2 * blocks * beams

    def spread(row):
        return jnp.where(inside, jnp.broadcast_to(row, (blocks, length)), 0.0)

    for order, term in enumerate(split(clean, 2)):
        for m in range(beams):
            base = cols * order + 2 * blocks * m
            pair = jnp.concatenate([spread(term[m : m + 1]), spread(term[beams + m : beams + m + 1])], 0)
            emb[base : base + 2 * blocks, :] = pair.astype(jnp.bfloat16)
    own = LAGS // nt
    half = own // 2
    groups = 4
    span = LAGS // groups
    targets = nt // groups
    real_lane = iota((span, 2 * cols), 1) % (2 * blocks) < blocks
    low_lane = iota((half, 2 * cols), 1) < cols

    def correlate(step, _):
        group = lax.rem(d // targets + groups // 2 + step, groups)

        sums = bdot_nt(lag_tab[pl.ds(pl.multiple_of(2 * TAPS + 4 * span * group, 2 * TAPS), 4 * span), :], emb[...])
        sums = sums[: 2 * span] + sums[2 * span :]
        sums = sums + pltpu.roll(sums, cols, 1)
        with_re, with_im = sums[:span], sums[span:]
        lagged = with_re + jnp.where(
            real_lane, pltpu.roll(with_im, 2 * cols - blocks, 1), -pltpu.roll(with_im, blocks, 1))
        for i in range(targets):
            lg[targets * group + i] = jnp.where(
                low_lane, lagged[own * i : own * i + half], lagged[own * i + half : own * (i + 1)])

        for i in range(targets):
            peer = targets * group + i

            @pl.when(peer != d)
            def _(peer=peer):
                lg_copy(peer, d).start()

        return 0

    lax.fori_loop(0, groups, correlate, 0)
    lg_buf[d] = lg[d]
    gm_all.wait_send()
    xm_all.wait_send()

    def rs_drain(j, _):
        peer = chip_peer(j)
        rs_copy(peer, peer).wait_send()
        return 0

    def core_drain(j, _):
        core_copy(j).wait_send()
        return 0

    for j in range(chips - 1):
        rs_drain(j, 0)
    lax.fori_loop(0, chips, core_drain, 0)
    lg_all.wait_recv()

    wide = 2 * blocks
    group = 128 // wide
    slot_of = iota((own, 128), 1) // wide
    upper_row = iota((own, 128), 0) < half

    def received(s):
        twice = jnp.concatenate([lg_buf[s], lg_buf[s]], 0)
        return jnp.where(upper_row, twice, pltpu.roll(twice, 64, 1))

    arrived = [received(s) for s in range(nt)]
    rows = []
    for m in range(beams):
        pieces = []
        for start in range(0, nt, group):
            acc = jnp.zeros((own, 128), jnp.float32)
            for s in range(group):
                moved = pltpu.roll(arrived[start + s], (wide * (s - m)) % 128, 1)
                acc = jnp.where(slot_of == s, moved, acc)
            pieces.append(acc)
        rows.append(jnp.concatenate(pieces, 1))
    stacked = jnp.concatenate(rows, 0)
    height = own * beams
    stacked_terms = jnp.concatenate(split(stacked, 2), 0).astype(jnp.bfloat16)
    table_copy.wait()
    spectrum = bdot(stacked_terms, table[0]) + bdot(stacked_terms, table[1])
    spectrum = spectrum[:height] + spectrum[height:]
    for m in range(beams):
        for part_id in range(2):
            out_ref[m, part_id] = spectrum[own * m : own * (m + 1), DOPPLER * part_id : DOPPLER * (part_id + 1)]

    lg_all.wait_send()


def doppler_table(blocks_total, blocks):
    q = np.arange(blocks_total)
    angle = 2.0 * np.pi * ((q[:, None] * np.arange(DOPPLER)[None, :]) % DOPPLER) / DOPPLER
    cosine, sine = np.cos(angle), np.sin(angle)
    first = np.concatenate([cosine, -sine], 1).reshape(-1, 1, blocks, 2 * DOPPLER)
    second = np.concatenate([sine, cosine], 1).reshape(-1, 1, blocks, 2 * DOPPLER)
    scale = 0.125 / math.sqrt(blocks_total * BLOCK)
    table = np.concatenate([first, second], 1).reshape(2 * blocks_total, 2 * DOPPLER) * scale
    head = table.astype(np.float32).astype(jnp.bfloat16)
    tail = (table - head.astype(np.float64)).astype(np.float32).astype(jnp.bfloat16)
    return np.stack([head, tail])


def on_device(ref_signal, surveillance, steering):
    nc, nt = lax.axis_size("chan"), lax.axis_size("tm")
    length = ref_signal.shape[1]
    chans = surveillance.shape[1]
    beams = steering.shape[1] // nc
    blocks = length // BLOCK
    own = LAGS // nt
    table = jnp.asarray(doppler_table(nt * blocks, blocks))
    vmem = pl.BlockSpec(memory_space=pltpu.VMEM)
    f32, bf16 = jnp.float32, jnp.bfloat16
    chips = nc // 2
    return pl.pallas_call(
        functools.partial(kernel, nc, nt),
        out_shape=jax.ShapeDtypeStruct((beams, 2, own, DOPPLER), f32),
        in_specs=[pl.BlockSpec(memory_space=pltpu.HBM)] * 4,
        out_specs=vmem,
        scratch_shapes=[
            pltpu.VMEM((2, length), f32),
            pltpu.VMEM((2, chans, length), f32),
            pltpu.VMEM((2, chans, beams * nc), f32),
            pltpu.VMEM((2, 2 * nt * blocks, 2 * DOPPLER), bf16),
            pltpu.VMEM((2, chips, 2 * beams, length), f32),
            pltpu.VMEM((chips, 2 * beams, length), f32),
            pltpu.VMEM((chips, 2 * beams, length), f32),
            pltpu.VMEM((chips, 2 * beams, length), f32),
            pltpu.VMEM((2, HALO), f32),
            pltpu.VMEM((2 * TAPS + 4 * LAGS, length), bf16),
            pltpu.VMEM((2, 2 * TAPS), f32),
            pltpu.VMEM((nt, 2, 2 * TAPS), f32),
            pltpu.VMEM((beams, 2 * TAPS), f32),
            pltpu.VMEM((nt, beams, 2 * TAPS), f32),
            pltpu.VMEM((TAPS, 2 * TAPS), f32),
            pltpu.VMEM((4 * blocks * beams, length), bf16),
            pltpu.VMEM((nt, own // 2, 128), f32),
            pltpu.VMEM((nt, own // 2, 128), f32),
            pltpu.SemaphoreType.REGULAR((3,)),
            pltpu.SemaphoreType.DMA,
            pltpu.SemaphoreType.DMA,
            pltpu.SemaphoreType.DMA((chips,)),
            pltpu.SemaphoreType.DMA((chips,)),
            pltpu.SemaphoreType.DMA((chips,)),
            pltpu.SemaphoreType.DMA((chips,)),
            pltpu.SemaphoreType.DMA,
            pltpu.SemaphoreType.DMA,
            pltpu.SemaphoreType.DMA,
            pltpu.SemaphoreType.DMA,
            pltpu.SemaphoreType.DMA,
            pltpu.SemaphoreType.DMA,
            pltpu.SemaphoreType.DMA((4,)),
        ],
        compiler_params=pltpu.CompilerParams(collective_id=0, has_side_effects=True, vmem_limit_bytes=60 << 20),
        name="radar",
    )(ref_signal, surveillance, jnp.swapaxes(steering, 1, 2), table)


def solution(mesh):
    placed = (P(None, "tm"), P(None, "chan", "tm"), P(None, None, "chan"))
    return jax.shard_map(
        on_device,
        mesh=mesh,
        in_specs=placed,
        out_specs=P("chan", None, "tm", None),
        check_vma=False,
    )
```

```python
import functools
import math

import jax
import jax.numpy as jnp
import numpy as np
from jax import lax
from jax.experimental import pallas as pl
from jax.experimental.pallas import tpu as pltpu
from jax.sharding import PartitionSpec as P

LAGS = 256
DOPPLER = 256
TAPS = 64
BLOCK = 256
HALO = 256
MESH = pl.DeviceIdType.MESH
HIGHEST = lax.Precision.HIGHEST


def dot(a, b):
    return lax.dot_general(a, b, (((1,), (0,)), ((), ())), precision=HIGHEST, preferred_element_type=jnp.float32)


def dot_nt(a, b):
    return lax.dot_general(a, b, (((1,), (1,)), ((), ())), precision=HIGHEST, preferred_element_type=jnp.float32)


def bdot(a, b):
    return lax.dot_general(a, b, (((1,), (0,)), ((), ())), preferred_element_type=jnp.float32)


def bdot_nt(a, b):
    return lax.dot_general(a, b, (((1,), (1,)), ((), ())), preferred_element_type=jnp.float32)


def split(x, terms):
    out = []
    for _ in range(terms):
        head = x.astype(jnp.bfloat16).astype(jnp.float32)
        out.append(head)
        x = x - head
    return out


def iota(shape, dim):
    return lax.broadcasted_iota(jnp.int32, shape, dim)


def conj_pack(a, b):
    half = a.shape[1] // 2
    sign = jnp.where(iota(a.shape, 1) < half, 1.0, -1.0)
    return sign * a + pltpu.roll(b, half, 1)


def widen(packed):
    half = packed.shape[1] // 2
    sign = jnp.where(iota(packed.shape, 1) < half, 1.0, -1.0)
    return jnp.concatenate([packed * sign, pltpu.roll(packed, half, 1)], 0)


def conj_product(left, right):
    n = left.shape[1] // 2
    pad = jnp.zeros((2 * n - left.shape[0], 2 * n), jnp.float32)
    square = dot(jnp.concatenate([left, pad], 0).T, jnp.concatenate([right, pad], 0))
    sign = jnp.where(iota((n, 2 * n), 1) < n, 1.0, -1.0)
    return square[:n] + sign * pltpu.roll(square[n:], n, 1)


def hermitian_inverse(m, scaled):
    n = m.shape[0]
    tile = 8
    blocks = [m[tile * i : tile * (i + 1)] for i in range(n // tile)]
    lane = iota((1, 2 * n), 1)
    row_id = iota((tile, 1), 0)
    flip = jnp.where(lane < n, -1.0, 1.0)
    for k in range(0, n, 2):
        home, at = blocks[k // tile], k % tile
        p0, p1 = home[at : at + 1], home[at + 1 : at + 2]
        a, br, bi = (jnp.broadcast_to(p0[:, j : j + 1], (1, 2 * n)) for j in (k, k + 1, n + k + 1))
        d = jnp.broadcast_to(p1[:, k + 1 : k + 2], (1, 2 * n))
        inv = 1.0 / (a * d - (br * br + bi * bi))
        at0, at1 = lane == k, lane == k + 1
        here = at0 | at1 | (lane == n + k) | (lane == n + k + 1)
        r0 = jnp.where(here, jnp.where(at0, 1.0, 0.0), p0)
        r1 = jnp.where(here, jnp.where(at1, 1.0, 0.0), p1)
        t0 = pltpu.roll(r0, n, 1) * flip
        t1 = pltpu.roll(r1, n, 1) * flip
        n0 = d * r0 - br * r1 - bi * t1
        u0 = d * t0 - br * t1 + bi * r1
        n1 = a * r1 - br * r0 + bi * t0
        u1 = a * t1 - br * t0 - bi * r0
        scaled[k : k + 1] = inv * n0
        scaled[k + 1 : k + 2] = inv * n1
        for i in range((k + 2) // tile, n // tile):
            block = blocks[i]
            c0r, c1r, c0i, c1i = (
                jnp.broadcast_to(block[:, j : j + 1], (tile, 2 * n)) for j in (k, k + 1, n + k, n + k + 1))
            change = (c0r * n0 + c1r * n1) + (c0i * u0 + c1i * u1)
            rest = jnp.where(here, 0.0, block) - inv * change
            blocks[i] = rest if tile * i > k + 1 else jnp.where(row_id > at + 1, rest, block)
    row = iota((n, 2 * n), 0)
    col = iota((n, 2 * n), 1) % n
    whole = jnp.concatenate(blocks, 0)
    lower = jnp.where(col < row - row % 2, whole, jnp.where(iota((n, 2 * n), 1) == row, 1.0, 0.0))
    return conj_product(lower, jnp.where(col < row - row % 2 + 2, scaled[...], 0.0))


def gram_matrix(g_row, e_row):
    n = TAPS
    row = iota((n, 2 * n), 0)
    lane = iota((n, 2 * n), 1)
    col = lane % n

    def shifted(v):
        return pltpu.roll(jnp.broadcast_to(v, (n, 2 * n)), 0, 1, stride=1, stride_axis=0)

    upper = jnp.where(col >= row, shifted(g_row), 0.0)
    flipped = jnp.concatenate([upper, jnp.zeros_like(upper)], 0).T
    lower = flipped[:n] - pltpu.roll(flipped[n:], n, 1)
    toeplitz = jnp.where(col >= row, upper, lower)
    tail = jnp.where((col >= row) & (row >= 1), shifted(e_row), 0.0)
    return toeplitz - conj_product(tail, tail)


def kernel(nc, nt, ref_hbm, surv_hbm, w_hbm, table_hbm, out_ref,
           ref_ref, surv_ref, w_ref, table, part, core_buf, chip_send, chip_buf, halo, lag_tab, gm, gm_buf, xm, xm_buf, scaled, emb, lg, lg_buf,
           reach, halo_ss, halo_rs, core_ss, core_rs, rs_ss, rs_rs, gm_ss, gm_rs, xm_ss, xm_rs, lg_ss, lg_rs, in_sems):
    c = lax.axis_index("chan")
    d = lax.axis_index("tm")
    length = ref_ref.shape[1]
    beams = part.shape[2] // 2
    chips = nc // 2
    core, chip = c % 2, c // 2
    partner = c + 1 - 2 * core
    blocks = length // BLOCK

    def tm_peer(j):
        return lax.rem(d + nt // 2 + (1 - 2 * (j % 2)) * ((j + 1) // 2) + nt, nt)

    def chan_peer(j):
        return lax.rem(c + 1 + j, nc)

    barrier = pltpu.get_barrier_semaphore()

    def greet_chan(j, _):
        pl.semaphore_signal(barrier, inc=1, device_id={"chan": chan_peer(j)}, device_id_type=MESH)
        return 0

    def tm_near(offset):
        return {"tm": lax.rem(d + offset + nt, nt)}

    for j in range(nc - 1):
        greet_chan(j, 0)
    for offset in (-2, -1, 1, 2):
        pl.semaphore_signal(barrier, inc=1, device_id=tm_near(offset), device_id_type=MESH)

    def reach_signal(i):
        for offset in (-(2 << i), 2 << i):
            pl.semaphore_signal(reach.at[i], inc=1, device_id=tm_near(offset), device_id_type=MESH)

    def reach_wait(i):
        pl.semaphore_wait(reach.at[i], 2)

    loads = [
        pltpu.make_async_copy(source, target, in_sems.at[i])
        for i, (source, target) in enumerate(
            ((w_hbm, w_ref), (surv_hbm, surv_ref), (ref_hbm, ref_ref), (table_hbm, table)))
    ]
    for load in loads:
        load.start()
    table_copy = loads.pop()
    for load in loads:
        load.wait()

    w_re, w_im = w_ref[0], w_ref[1]
    weights_t = jnp.concatenate(
        [jnp.concatenate([w_re, w_im], 1), jnp.concatenate([-w_im, w_re], 1)], 0)
    w_hi, w_mid, w_lo = split(weights_t, 3)
    survey = jnp.concatenate([surv_ref[0], surv_ref[1]], 0)
    s_hi, s_mid, s_lo = split(survey, 3)
    left = jnp.concatenate([w_hi, w_hi, w_mid, w_hi, w_mid, w_lo], 0)
    depth = left.shape[0]
    left = jnp.concatenate([left, jnp.zeros((256 - depth, left.shape[1]), jnp.float32)], 0).T
    right_side = jnp.concatenate(
        [s_hi, s_mid, s_hi, s_lo, s_mid, s_hi, jnp.zeros((256 - depth, length), jnp.float32)], 0)
    partial = bdot(left.astype(jnp.bfloat16), right_side.astype(jnp.bfloat16))
    part_re, part_im = partial[: beams * nc], partial[beams * nc :]
    for owner in range(nc):
        rows = slice(beams * owner, beams * (owner + 1))
        part[owner % 2, owner // 2] = jnp.concatenate([part_re[rows], part_im[rows]], 0)

    pl.semaphore_wait(barrier, nc - 1 + 4)
    reach_signal(0)

    right = lax.rem(d + 1, nt)
    halo_copy = pltpu.make_async_remote_copy(
        src_ref=ref_ref.at[:, pl.ds(length - HALO, HALO)], dst_ref=halo, send_sem=halo_ss, recv_sem=halo_rs,
        device_id={"tm": right}, device_id_type=MESH)
    halo_copy.start()

    halves = 2
    steps = chips // halves
    far_first = sorted(
        ((a, b) for a in range(halves) for b in range(steps) if a or b),
        key=lambda ab: -(2 * ab[0] + min(ab[1], steps - ab[1])))

    def chip_peer(j):
        a, b = far_first[j]
        return lax.rem(chip // steps + a, halves) * steps + lax.rem(chip % steps + b, steps)

    def core_copy(j):
        return pltpu.make_async_remote_copy(
            src_ref=part.at[1 - core, j], dst_ref=core_buf.at[j], send_sem=core_ss.at[j], recv_sem=core_rs.at[j],
            device_id={"chan": partner}, device_id_type=MESH)

    def rs_copy(peer, slot):
        return pltpu.make_async_remote_copy(
            src_ref=chip_send.at[peer], dst_ref=chip_buf.at[slot], send_sem=rs_ss.at[peer], recv_sem=rs_rs.at[slot],
            device_id={"chan": 2 * peer + core}, device_id_type=MESH)

    def core_start(j, _):
        core_copy(chip_peer(j)).start()
        return 0

    for j in range(chips - 1):
        core_start(j, 0)
    core_copy(chip).start()

    def rs_start(j, _):
        peer = chip_peer(j)
        core_copy(peer).wait_recv()
        chip_send[peer] = part[core, peer] + core_buf[peer]
        rs_copy(peer, chip).start()
        return 0

    reach_wait(0)
    reach_signal(1)

    for j in range(chips - 1):
        rs_start(j, 0)

    halo_copy.wait()
    ref = ref_ref[...]
    before = jnp.where(d == 0, 0.0, halo[...])
    extended = jnp.concatenate([before, ref], 1)

    def lags_of(p, first, count):
        row = jnp.broadcast_to(extended[p : p + 1, :], (count, HALO + length))
        return pltpu.roll(row, first, 1, stride=1, stride_axis=0)[:, HALO:]

    taps = jnp.concatenate([lags_of(0, 0, TAPS), lags_of(1, 0, TAPS)], 0)
    taps_hi, taps_mid, taps_lo = split(taps, 3)
    for order, term in enumerate((taps_lo, taps_hi, taps_mid)):
        lag_tab[2 * TAPS * order : 2 * TAPS * (order + 1)] = term.astype(jnp.bfloat16)

    reach_wait(1)
    reach_signal(2)
    core_copy(chip).wait_recv()
    chip_buf[chip] = part[core, chip] + core_buf[chip]

    tap_rows = 6 * TAPS

    def lag_products(rows8):
        terms = jnp.concatenate(split(rows8, 3), 0).astype(jnp.bfloat16)
        cols = bdot_nt(lag_tab[:tap_rows], terms)
        cols = cols[: 2 * TAPS] + cols[2 * TAPS : 4 * TAPS] + cols[4 * TAPS :]
        turned = jnp.concatenate([cols, jnp.zeros((2 * TAPS, 128 - cols.shape[1]), jnp.float32)], 1).T
        return turned[:8] + turned[8:16] + turned[16:24]

    row8 = iota((8, length), 0)
    mark = jnp.where((iota((8, length), 1) == length - 1) & (d == nt - 1), 1.0, 0.0)
    probe = jnp.where(row8 == 0, ref[0:1], jnp.where(row8 == 1, ref[1:2], jnp.where(row8 == 2, mark, 0.0)))
    g_raw = lag_products(probe)
    g_conj = conj_pack(g_raw[0:1], g_raw[1:2])
    gm[0:1, :] = jnp.where(iota(g_conj.shape, 1) < TAPS, g_conj, -g_conj)
    gm[1:2, :] = g_raw[2:3]

    def gm_copy(peer, slot):
        return pltpu.make_async_remote_copy(
            src_ref=gm, dst_ref=gm_buf.at[slot], send_sem=gm_ss, recv_sem=gm_rs,
            device_id={"tm": peer}, device_id_type=MESH)

    def xm_copy(peer, slot):
        return pltpu.make_async_remote_copy(
            src_ref=xm, dst_ref=xm_buf.at[slot], send_sem=xm_ss, recv_sem=xm_rs,
            device_id={"tm": peer}, device_id_type=MESH)

    def lg_copy(peer, slot):
        return pltpu.make_async_remote_copy(
            src_ref=lg.at[peer], dst_ref=lg_buf.at[slot], send_sem=lg_ss, recv_sem=lg_rs,
            device_id={"tm": peer}, device_id_type=MESH)

    def tm_start(copy):
        for j in range(nt - 1):
            copy(tm_peer(j), d).start()

    def all_of(buf, send_sem, recv_sem):
        return pltpu.make_async_remote_copy(
            src_ref=buf.at[pl.ds(0, nt - 1)], dst_ref=buf.at[pl.ds(0, nt - 1)], send_sem=send_sem, recv_sem=recv_sem,
            device_id={"tm": tm_peer(0)}, device_id_type=MESH)

    gm_all = all_of(gm_buf, gm_ss, gm_rs)
    xm_all = all_of(xm_buf, xm_ss, xm_rs)
    lg_all = all_of(lg_buf, lg_ss, lg_rs)

    reach_wait(2)
    tm_start(gm_copy)
    gm_buf[d] = gm[...]

    def rs_wait(j, _):
        peer = chip_peer(j)
        rs_copy(peer, peer).wait_recv()
        return 0

    total = chip_buf[chip]
    for j in reversed(range(chips - 1)):
        rs_wait(j, 0)
        total = total + chip_buf[chip_peer(j)]

    x_raw = lag_products(total)
    xm[...] = conj_pack(x_raw[:beams], x_raw[beams:])
    tm_start(xm_copy)
    xm_buf[d] = xm[...]

    for p in range(2):
        hi, mid = split(lags_of(p, TAPS, LAGS - TAPS), 2)
        for group in range(1, LAGS // TAPS):
            rows = slice(TAPS * (group - 1), TAPS * group)
            base = 2 * TAPS + 4 * TAPS * group + TAPS * p
            lag_tab[base : base + TAPS] = hi[rows].astype(jnp.bfloat16)
            lag_tab[base + 2 * TAPS : base + 3 * TAPS] = mid[rows].astype(jnp.bfloat16)

    gm_all.wait_recv()
    g_sum = jnp.sum(gm_buf[...], axis=0)
    gram = gram_matrix(g_sum[0:1], g_sum[1:2])
    level = 1.0 / gram[0:1, 0:1]
    gram = gram * level
    inverse = widen(hermitian_inverse(gram, scaled))
    gram_wide = widen(gram)

    xm_all.wait_recv()
    x = jnp.sum(xm_buf[...], axis=0) * level
    weights = dot(x, inverse)
    weights = weights + dot(x - dot(weights, gram_wide), inverse)

    sign = jnp.where(iota(weights.shape, 1) < TAPS, 1.0, -1.0)
    both = jnp.concatenate([weights * sign, pltpu.roll(weights, TAPS, 1)], 0)
    both_terms = jnp.concatenate(split(both, 3), 0).astype(jnp.bfloat16)
    model = bdot(jnp.concatenate([both_terms] * 3, 1), lag_tab[:tap_rows])
    clean = total - (model[: 2 * beams] + model[2 * beams : 4 * beams] + model[4 * beams : 6 * beams])

    inside = iota((blocks, length), 1) // BLOCK == iota((blocks, length), 0)
    cols = 2 * blocks * beams

    def spread(row):
        return jnp.where(inside, jnp.broadcast_to(row, (blocks, length)), 0.0)

    for order, term in enumerate(split(clean, 2)):
        for m in range(beams):
            base = cols * order + 2 * blocks * m
            pair = jnp.concatenate([spread(term[m : m + 1]), spread(term[beams + m : beams + m + 1])], 0)
            emb[base : base + 2 * blocks, :] = pair.astype(jnp.bfloat16)
    own = LAGS // nt
    half = own // 2
    groups = 4
    span = LAGS // groups
    targets = nt // groups
    real_lane = iota((span, 2 * cols), 1) % (2 * blocks) < blocks
    low_lane = iota((half, 2 * cols), 1) < cols

    def correlate(step, _):
        group = lax.rem(d // targets + groups // 2 + step, groups)

        sums = bdot_nt(lag_tab[pl.ds(pl.multiple_of(2 * TAPS + 4 * span * group, 2 * TAPS), 4 * span), :], emb[...])
        sums = sums[: 2 * span] + sums[2 * span :]
        sums = sums + pltpu.roll(sums, cols, 1)
        with_re, with_im = sums[:span], sums[span:]
        lagged = with_re + jnp.where(
            real_lane, pltpu.roll(with_im, 2 * cols - blocks, 1), -pltpu.roll(with_im, blocks, 1))
        for i in range(targets):
            lg[targets * group + i] = jnp.where(
                low_lane, lagged[own * i : own * i + half], lagged[own * i + half : own * (i + 1)])

        for i in range(targets):
            peer = targets * group + i

            @pl.when(peer != d)
            def _(peer=peer):
                lg_copy(peer, d).start()

        return 0

    lax.fori_loop(0, groups, correlate, 0)
    lg_buf[d] = lg[d]
    gm_all.wait_send()
    xm_all.wait_send()

    def rs_drain(j, _):
        peer = chip_peer(j)
        rs_copy(peer, peer).wait_send()
        return 0

    def core_drain(j, _):
        core_copy(j).wait_send()
        return 0

    for j in range(chips - 1):
        rs_drain(j, 0)
    lax.fori_loop(0, chips, core_drain, 0)
    lg_all.wait_recv()

    wide = 2 * blocks
    group = 128 // wide
    slot_of = iota((own, 128), 1) // wide
    upper_row = iota((own, 128), 0) < half

    def received(s):
        twice = jnp.concatenate([lg_buf[s], lg_buf[s]], 0)
        return jnp.where(upper_row, twice, pltpu.roll(twice, 64, 1))

    arrived = [received(s) for s in range(nt)]
    rows = []
    for m in range(beams):
        pieces = []
        for start in range(0, nt, group):
            acc = jnp.zeros((own, 128), jnp.float32)
            for s in range(group):
                moved = pltpu.roll(arrived[start + s], (wide * (s - m)) % 128, 1)
                acc = jnp.where(slot_of == s, moved, acc)
            pieces.append(acc)
        rows.append(jnp.concatenate(pieces, 1))
    stacked = jnp.concatenate(rows, 0)
    height = own * beams
    stacked_terms = jnp.concatenate(split(stacked, 2), 0).astype(jnp.bfloat16)
    table_copy.wait()
    spectrum = bdot(stacked_terms, table[0]) + bdot(stacked_terms, table[1])
    spectrum = spectrum[:height] + spectrum[height:]
    for m in range(beams):
        for part_id in range(2):
            out_ref[m, part_id] = spectrum[own * m : own * (m + 1), DOPPLER * part_id : DOPPLER * (part_id + 1)]

    lg_all.wait_send()


def doppler_table(blocks_total, blocks):
    q = np.arange(blocks_total)
    angle = 2.0 * np.pi * ((q[:, None] * np.arange(DOPPLER)[None, :]) % DOPPLER) / DOPPLER
    cosine, sine = np.cos(angle), np.sin(angle)
    first = np.concatenate([cosine, -sine], 1).reshape(-1, 1, blocks, 2 * DOPPLER)
    second = np.concatenate([sine, cosine], 1).reshape(-1, 1, blocks, 2 * DOPPLER)
    scale = 0.125 / math.sqrt(blocks_total * BLOCK)
    table = np.concatenate([first, second], 1).reshape(2 * blocks_total, 2 * DOPPLER) * scale
    head = table.astype(np.float32).astype(jnp.bfloat16)
    tail = (table - head.astype(np.float64)).astype(np.float32).astype(jnp.bfloat16)
    return np.stack([head, tail])


def on_device(ref_signal, surveillance, steering):
    nc, nt = lax.axis_size("chan"), lax.axis_size("tm")
    length = ref_signal.shape[1]
    chans = surveillance.shape[1]
    beams = steering.shape[1] // nc
    blocks = length // BLOCK
    own = LAGS // nt
    table = jnp.asarray(doppler_table(nt * blocks, blocks))
    vmem = pl.BlockSpec(memory_space=pltpu.VMEM)
    f32, bf16 = jnp.float32, jnp.bfloat16
    chips = nc // 2
    return pl.pallas_call(
        functools.partial(kernel, nc, nt),
        out_shape=jax.ShapeDtypeStruct((beams, 2, own, DOPPLER), f32),
        in_specs=[pl.BlockSpec(memory_space=pltpu.HBM)] * 4,
        out_specs=vmem,
        scratch_shapes=[
            pltpu.VMEM((2, length), f32),
            pltpu.VMEM((2, chans, length), f32),
            pltpu.VMEM((2, chans, beams * nc), f32),
            pltpu.VMEM((2, 2 * nt * blocks, 2 * DOPPLER), bf16),
            pltpu.VMEM((2, chips, 2 * beams, length), f32),
            pltpu.VMEM((chips, 2 * beams, length), f32),
            pltpu.VMEM((chips, 2 * beams, length), f32),
            pltpu.VMEM((chips, 2 * beams, length), f32),
            pltpu.VMEM((2, HALO), f32),
            pltpu.VMEM((2 * TAPS + 4 * LAGS, length), bf16),
            pltpu.VMEM((2, 2 * TAPS), f32),
            pltpu.VMEM((nt, 2, 2 * TAPS), f32),
            pltpu.VMEM((beams, 2 * TAPS), f32),
            pltpu.VMEM((nt, beams, 2 * TAPS), f32),
            pltpu.VMEM((TAPS, 2 * TAPS), f32),
            pltpu.VMEM((4 * blocks * beams, length), bf16),
            pltpu.VMEM((nt, own // 2, 128), f32),
            pltpu.VMEM((nt, own // 2, 128), f32),
            pltpu.SemaphoreType.REGULAR((3,)),
            pltpu.SemaphoreType.DMA,
            pltpu.SemaphoreType.DMA,
            pltpu.SemaphoreType.DMA((chips,)),
            pltpu.SemaphoreType.DMA((chips,)),
            pltpu.SemaphoreType.DMA((chips,)),
            pltpu.SemaphoreType.DMA((chips,)),
            pltpu.SemaphoreType.DMA,
            pltpu.SemaphoreType.DMA,
            pltpu.SemaphoreType.DMA,
            pltpu.SemaphoreType.DMA,
            pltpu.SemaphoreType.DMA,
            pltpu.SemaphoreType.DMA,
            pltpu.SemaphoreType.DMA((4,)),
        ],
        compiler_params=pltpu.CompilerParams(collective_id=0, has_side_effects=True, vmem_limit_bytes=60 << 20),
        name="radar",
    )(ref_signal, surveillance, jnp.swapaxes(steering, 1, 2), table)


def solution(mesh):
    placed = (P(None, "tm"), P(None, "chan", "tm"), P(None, None, "chan"))
    return jax.shard_map(
        on_device,
        mesh=mesh,
        in_specs=placed,
        out_specs=P("chan", None, "tm", None),
        check_vma=False,
    )
```
